128 devices in a mesh: kvh: 4 (over z), page: 32 (over x, y, core).
Axes of the slice: x: 4, y: 4, z: 4, core: 2. Of those that a mesh axis runs over, the one named last changes fastest.
Arguments:
- queries: bfloat16 [128, 128, 128], P('page', 'kvh'), may hold values from -8 to 8
- group_ids: int32 [128], replicated, may hold values from 0 to 3, never falling along the last dimension, each value on 1 to 64 neighbouring positions
- suffix_lengths: int32 [128], P('page'), may hold values from 1 to 512, as said below
- block_tables: int32 [128, 8], P('page'), may hold values from 0 to 1023, as said below
- prefix_keys: bfloat16 [4, 32768, 8, 128], P(None, 'page', 'kvh'), may hold values from -8 to 8
- prefix_values: bfloat16 [4, 32768, 8, 128], P(None, 'page', 'kvh'), may hold values from -4 to 4
- suffix_keys: bfloat16 [1024, 64, 8, 128], P('page', None, 'kvh'), may hold values from -8 to 8
- suffix_values: bfloat16 [1024, 64, 8, 128], P('page', None, 'kvh'), may hold values from -4 to 4
- out_weight: bfloat16 [16384, 16384], P('kvh', 'page'), may hold values from -6 to 6
Outputs:
- layer_out: bfloat16 [128, 16384], P('kvh', 'page')
The draws below stay inside these ranges and needn't reach their ends.
Inputs may be any that keep to these rules, and one draw needn't show every extreme that they name: `suffix_lengths`: suffix lengths are at least 1 and at most 512, which some row reaches. `block_tables`: the entries of row r are distinct pages of the pool block held with row r, numbers from (r // 4) * 32 to (r // 4 + 1) * 32 - 1.
All inputs are finite; a program needn't handle non-finite values.
Results may differ from the reference program's by a relative error of at most 0.023.
Values may be sent and summed in bfloat16 or wider, within the bound.
A program may use at most 192 MiB of HBM per device.

```python
import math
import jax
import jax.numpy as jnp
import numpy as np
from jax import lax

D = 16384
HEADS = 128
KV_HEADS = 8
HD = 128
PAGE_LEN = 64
GROUPS = 4
ROWS_DEV = 4
SUF_PAGES = 8
ROWS = 128
GROUP_MOST = 64
PREFIX = 32768
POOL = 1024


def signs(key):
    bits = jax.random.randint(jax.random.fold_in(key, 7), (KV_HEADS, HD), 0, 2)
    return jnp.where(bits == 1, 8.0, -8.0).astype(jnp.float32)


def draw_prefix_keys(key, part):
    shape = (GROUPS, PREFIX, KV_HEADS, HD)
    base = jnp.clip(0.5 * jax.random.normal(jax.random.fold_in(key, 1), shape, jnp.float32), -2.0, 2.0)
    pattern = signs(key)
    first = (PREFIX // 3 + 5) % PREFIX
    second = (2 * PREFIX // 3 + 7) % PREFIX
    base = base.at[:, first].set(jnp.broadcast_to(pattern, (GROUPS, KV_HEADS, HD)))
    base = base.at[:, second].set(jnp.broadcast_to(0.99 * pattern, (GROUPS, KV_HEADS, HD)))
    return base.astype(jnp.bfloat16)


def draw_queries(key, part):
    shape = (ROWS, HEADS, HD)
    base = jnp.clip(3.0 * jax.random.normal(jax.random.fold_in(key, 2), shape, jnp.float32), -8.0, 8.0)
    aligned = jnp.repeat(signs(key), HEADS // KV_HEADS, axis=0) / 8.0
    row_index = jnp.arange(ROWS)
    target = 110.0 + 70.0 * (row_index % 3).astype(jnp.float32)
    strength = target / (8.0 * jnp.sqrt(jnp.float32(HD)))
    chosen = row_index % 5 == 0
    return jnp.where(chosen[:, None, None], strength[:, None, None] * aligned[None], base).astype(jnp.bfloat16)


def draw_suffix_lengths(key, part):
    most = SUF_PAGES * PAGE_LEN
    short = jax.random.randint(jax.random.fold_in(key, 11), (ROWS,), 1, most // 4 + 1)
    longer = jax.random.randint(jax.random.fold_in(key, 12), (ROWS,), most // 2, most + 1)
    pick = jax.random.randint(jax.random.fold_in(key, 13), (ROWS,), 0, 4) == 0
    lengths = jnp.where(pick, longer, short)
    spot = jax.random.randint(jax.random.fold_in(key, 14), (), 0, ROWS)
    return lengths.at[spot].set(most).astype(jnp.int32)


def draw_block_tables(key, part):
    owners = ROWS // ROWS_DEV
    pool_dev = ROWS_DEV * SUF_PAGES
    keys = jax.random.split(jax.random.fold_in(key, 21), owners)
    perms = jax.vmap(lambda k: jax.random.permutation(k, pool_dev))(keys)
    perms = perms + (jnp.arange(owners) * pool_dev)[:, None]
    return perms.reshape(ROWS, SUF_PAGES).astype(jnp.int32)


def shard_levels(stream_key, extent, shards, smallest, high):
    def one(dim, parts):
        draws = jax.random.uniform(jax.random.fold_in(jax.random.fold_in(stream_key, 6), dim), (parts,), jnp.float32, smallest / len(shards), high / len(shards))
        return jnp.repeat(jnp.exp(draws), extent[dim] // parts).reshape((-1,) + (1,) * (len(extent) - dim - 1))

    factor_of = one(*shards[0])
    for cut in shards[1:]:
        factor_of = factor_of * one(*cut)
    return factor_of


def split_up(number_of, total, reach, slope):
    loads = [(1 << 20) // math.isqrt(grade ** slope) + 1 for grade in range(2, number_of + 1)]
    surplus, holding = total - reach - (number_of - 1), [1] * (number_of - 1)
    while surplus > 0:
        movable = [i for i in range(number_of - 1) if holding[i] < reach]
        whole, remaining = sum([loads[i] for i in movable]), surplus
        for i in movable:
            extra = min(reach - holding[i], max(1, remaining * loads[i] // whole), surplus)
            holding[i] = holding[i] + extra
            surplus = surplus - extra
    return np.array([reach] + holding)


def ragged_sizes(key, count, total, bound, skew):
    if count == 2:
        one = jax.random.randint(key, (), max(1, total - bound), min(bound, total - 1) + 1)
        return jnp.stack([one, total - one])
    sizes = jnp.asarray(split_up(count, total, bound, skew), jnp.int32)
    twos = (count - 1) // 2
    donor, sink = sizes[1:1 + 2 * twos:2], sizes[2:2 + 2 * twos:2]
    margin = jnp.minimum(donor - 1, bound - sink)
    passed = jax.random.randint(jax.random.fold_in(key, 1), (twos,), 0, 1 << 20) % (margin + 1)
    sizes = sizes.at[1:1 + 2 * twos:2].set(donor - passed).at[2:2 + 2 * twos:2].set(sink + passed)
    return sizes[jax.random.permutation(jax.random.fold_in(key, 2), count)]


def normal_values(key, shape, spread, most, pieces=(), kind=jnp.bfloat16):
    loudness = shard_levels(key, shape, pieces, -0.22, 0.18) if pieces else 1.0
    array = jax.random.normal(key, shape, jnp.float32) * spread * loudness
    return jnp.minimum(jnp.maximum(array, -most), most).astype(kind)


def setup_inputs(seed: int = 0) -> dict:
    splits = jax.random.split(jax.random.key(seed), 10)
    queries = draw_queries(jax.random.fold_in(splits[9], 71), 0)
    group_ids = jnp.searchsorted(jnp.cumsum(ragged_sizes(splits[1], GROUPS, ROWS, GROUP_MOST, 2)), jnp.arange(ROWS), side="right").astype(jnp.int32)
    suffix_lengths = draw_suffix_lengths(jax.random.fold_in(splits[9], 71), 0)
    block_tables = draw_block_tables(jax.random.fold_in(splits[9], 71), 0)
    prefix_keys = draw_prefix_keys(jax.random.fold_in(splits[9], 71), 0)
    prefix_values = normal_values(splits[5], (GROUPS, PREFIX, KV_HEADS, HD), 1.0, 4.0, ((1, 32), (2, 4)))
    suffix_keys = normal_values(splits[6], (POOL, PAGE_LEN, KV_HEADS, HD), 0.8, 8.0, ((0, 32), (2, 4)))
    suffix_values = normal_values(splits[7], (POOL, PAGE_LEN, KV_HEADS, HD), 1.0, 4.0, ((0, 32), (2, 4)))
    out_weight = normal_values(splits[8], (HEADS * HD, D), (max(1, HEADS * HD // PREFIX)) ** -0.5, 6.0, ((0, 4), (1, 32)))
    return {"queries": queries, "group_ids": group_ids, "suffix_lengths": suffix_lengths, "block_tables": block_tables, "prefix_keys": prefix_keys, "prefix_values": prefix_values, "suffix_keys": suffix_keys, "suffix_values": suffix_values, "out_weight": out_weight}


def reference(queries, group_ids, suffix_lengths, block_tables, prefix_keys, prefix_values, suffix_keys, suffix_values, out_weight):
    per_kv = HEADS // KV_HEADS
    scale = HD ** -0.5
    suffix_span = SUF_PAGES * PAGE_LEN

    def one_row(items):
        query, group, length, table = items
        q_heads = query.astype(jnp.float32).reshape(KV_HEADS, per_kv, HD)
        keys = lax.dynamic_index_in_dim(prefix_keys, group, 0, keepdims=False).astype(jnp.float32)
        values = lax.dynamic_index_in_dim(prefix_values, group, 0, keepdims=False).astype(jnp.float32)
        tail_keys = suffix_keys[table].reshape(suffix_span, KV_HEADS, HD).astype(jnp.float32)
        tail_values = suffix_values[table].reshape(suffix_span, KV_HEADS, HD).astype(jnp.float32)
        all_keys = jnp.concatenate([keys, tail_keys], axis=0)
        all_values = jnp.concatenate([values, tail_values], axis=0)
        scores = jnp.einsum("kqd,tkd->kqt", q_heads, all_keys) * scale
        live = jnp.concatenate([jnp.ones((PREFIX,), bool), jnp.arange(suffix_span) < length])
        scores = jnp.where(live[None, None, :], scores, jnp.float32(-1e30))
        top = jnp.max(scores, axis=-1)
        weights = jnp.exp(scores - top[..., None])
        total = jnp.sum(weights, axis=-1)
        rounded = lax.optimization_barrier(weights.astype(jnp.bfloat16)).astype(jnp.float32)
        mixed = jnp.einsum("kqt,tkd->kqd", rounded, all_values) / total[..., None]
        return mixed.astype(jnp.bfloat16).reshape(HEADS * HD)

    attn = lax.map(one_row, (queries, group_ids, suffix_lengths, block_tables))
    return jnp.dot(attn, out_weight, preferred_element_type=jnp.float32).astype(jnp.bfloat16)
```

```python
import functools
import math

import jax
import jax.numpy as jnp
from jax import lax
from jax.experimental import pallas as pl
from jax.experimental.pallas import tpu as pltpu
from jax.sharding import PartitionSpec as P

MESH = pl.DeviceIdType.MESH
F32 = jnp.float32
BF16 = jnp.bfloat16
LOW = -1e30


def nt_dot(a, b):
    return lax.dot_general(a, b, (((1,), (1,)), ((), ())), preferred_element_type=F32)


def kernel(
    pages, zs, dims,
    gid, slen, tab, q_in, pk, pv, sk, sv, w_in, out,
    qv, q_all, kraw, vraw, stage, kd, vd, kr, vr, skv, svv, wl, wr, s_ref,
    acc_s, m_s, l_s, sendb, recvb, sfx, sfx_in, smc, slc, coef, fin, attn_all, a_mat, pf, part, pin,
    loc, q_ss, q_rs, kv_ss, kv_rs, w_ss, w_rs, x_ss, x_rs, o_ss, o_rs, a_ss, a_rs, p_ss, p_rs,
):
    rows, per_kv, hd, tokens, groups, sufp = dims
    chips = pages // 2
    lanes = 2 * rows * per_kv
    c2 = hd ** (-0.5) * math.log2(math.e)
    me = lax.axis_index("page")
    z = lax.axis_index("kvh")
    chip = me // 2
    core = me % 2
    other = 1 - core
    sib = chip * 2 + other

    def to_page(src, dst, ss, rs, page):
        return pltpu.make_async_remote_copy(
            src_ref=src, dst_ref=dst, send_sem=ss, recv_sem=rs,
            device_id={"page": page}, device_id_type=MESH)

    loads = [
        pltpu.make_async_copy(q_in, qv, loc.at[0]),
        pltpu.make_async_copy(sk, skv, loc.at[1]),
        pltpu.make_async_copy(sv, svv, loc.at[2]),
        pltpu.make_async_copy(w_in.at[pl.ds(core * wl.shape[0], wl.shape[0])], wl, loc.at[3]),
        pltpu.make_async_copy(q_in.at[:, pl.ds(core * per_kv, per_kv)], q_all.at[chip, core], loc.at[4]),
    ]
    kvl = []
    for g in range(groups):
        kvl.append(pltpu.make_async_copy(pk.at[g], kraw.at[g], loc.at[6 + 2 * g]))
        kvl.append(pltpu.make_async_copy(pv.at[g], vraw.at[g], loc.at[7 + 2 * g]))
    for copy in [loads[0], loads[4]] + kvl + loads[1:4]:
        copy.start()

    bar = pltpu.get_barrier_semaphore()

    @pl.loop(1, pages)
    def _(j):
        pl.semaphore_signal(bar, inc=1, device_id={"page": (me + j) % pages}, device_id_type=MESH)

    @pl.loop(1, zs)
    def _(j):
        for cc in range(2):
            pl.semaphore_signal(
                bar, inc=1, device_id={"kvh": (z + j) % zs, "page": chip * 2 + cc}, device_id_type=MESH)

    pl.semaphore_wait(bar, pages - 1 + 2 * (zs - 1))

    def q_copy(page, src_page):
        kv = page % 2
        return to_page(
            q_in.at[:, pl.ds(kv * per_kv, per_kv)], q_all.at[src_page // 2, src_page % 2],
            q_ss.at[page], q_rs.at[src_page], page)

    @pl.loop(1, pages)
    def _(j):
        q_copy((me + j) % pages, me).start()

    def count(r, c):
        g = gid[r]
        return tuple(c[e] + (g <= e).astype(jnp.int32) for e in range(groups - 1))

    first = lax.fori_loop(0, rows * pages, count, (jnp.int32(0),) * (groups - 1))
    btile = [jnp.minimum(f // (2 * rows), chips - 1) for f in first]

    def kv_copy(g, i):
        return to_page((kd, vd)[i].at[g, other], (kr, vr)[i].at[g], kv_ss.at[2 * g + i], kv_rs.at[2 * g + i], sib)

    for g in range(groups):
        for i in range(2):
            kvl[2 * g + i].wait()
            stage[...] = (kraw, vraw)[i][g].astype(F32)
            for kv in range(2):
                (kd, vd)[i][g, kv] = stage[pl.ds(kv, tokens, stride=2), :].astype(BF16)
            kv_copy(g, i).start()

    def w_copy():
        return to_page(w_in.at[pl.ds(other * wl.shape[0], wl.shape[0])], wr, w_ss, w_rs, sib)

    w_copy().start()

    span = sufp * skv.shape[1]
    both = 2 * per_kv
    col = lax.broadcasted_iota(jnp.int32, (both, span), 1)
    row = lax.broadcasted_iota(jnp.int32, (both, span), 0)
    mine = (col % 2) == (row // per_kv)
    token = col // 2
    for copy in loads[:3]:
        copy.wait()
    for r in range(rows):
        pgs = [tab[r, j] % skv.shape[0] for j in range(sufp)]
        keys = jnp.concatenate([skv[pg] for pg in pgs], axis=0)
        vals = jnp.concatenate([svv[pg] for pg in pgs], axis=0)
        live = mine & (token < slen[r])
        s = jnp.where(live, nt_dot(qv[r], keys) * c2, LOW)
        top = jnp.max(s, axis=1, keepdims=True)
        p = jnp.where(live, jnp.exp2(s - top), 0.0)
        tot = jnp.sum(p, axis=1, keepdims=True)
        o = jnp.dot(p.astype(BF16), vals, preferred_element_type=F32)
        for kv in range(2):
            a, b = kv * per_kv, (kv + 1) * per_kv
            sfx[kv, r * per_kv:(r + 1) * per_kv, :] = o[a:b]
            smc[kv, r * per_kv:(r + 1) * per_kv, :] = jnp.broadcast_to(top[a:b], (per_kv, 128))
            slc[kv, r * per_kv:(r + 1) * per_kv, :] = jnp.broadcast_to(tot[a:b], (per_kv, 128))
    half = rows * per_kv
    hrow = lax.broadcasted_iota(jnp.int32, (half, 128), 0) + core * half
    hlane = lax.broadcasted_iota(jnp.int32, (half, 128), 1)
    sub8 = lax.broadcasted_iota(jnp.int32, (8, 128), 0)
    lane8 = lax.broadcasted_iota(jnp.int32, (8, 128), 1)
    held = (lane8 // half) == core
    for kv in range(2):
        mrow = jnp.sum(jnp.where(hrow == hlane, smc[kv], 0.0), axis=0, keepdims=True)
        lrow = jnp.sum(jnp.where(hrow == hlane, slc[kv], 0.0), axis=0, keepdims=True)
        block = jnp.where(sub8 == 0, mrow, jnp.where(sub8 == 1, lrow, 0.0))
        sfx[kv, half:half + 8, :] = jnp.where(held, block, jnp.where(sub8 == 0, LOW, 0.0))

    def x_copy():
        return to_page(sfx.at[other], sfx_in, x_ss, x_rs, sib)

    x_copy().start()

    loads[4].wait()

    @pl.loop(1, pages)
    def _(j):
        q_copy(me, (me + j) % pages).wait_recv()

    for g in range(groups):
        for i in range(2):
            kv_copy(g, i).wait_recv()

    def o_copy(dst_chip, src_chip):
        return to_page(sendb.at[dst_chip], recvb.at[src_chip], o_ss.at[dst_chip], o_rs.at[src_chip], dst_chip * 2 + core)

    prow = lax.broadcasted_iota(jnp.int32, (lanes, 128), 0)
    plane = lax.broadcasted_iota(jnp.int32, (lanes, 128), 1)
    nb = groups - 1

    def step(s, carry):
        t = (chip + 1 + jnp.maximum(s - nb, 0)) % chips
        qt = t
        for e in range(nb):
            qt = jnp.where(s == e, btile[e], qt)
        g_low = gid[t * (2 * rows)]
        g = jnp.where(s < nb, s + 1, g_low)
        slot = jnp.minimum(s, nb)
        q = q_all[qt].reshape(lanes, hd)
        s_ref[:, :tokens] = nt_dot(q, kd[g, core])
        s_ref[:, tokens:] = nt_dot(q, kr[g])
        x = s_ref[...]
        top = (jnp.max(x, axis=1, keepdims=True) * c2).astype(BF16).astype(F32)
        p = jnp.exp2(x * c2 - top)
        tot = jnp.sum(p, axis=1, keepdims=True)
        pb = p.astype(BF16)
        o = jnp.dot(pb[:, :tokens], vd[g, core], preferred_element_type=F32)
        o += jnp.dot(pb[:, tokens:], vr[g], preferred_element_type=F32)
        acc_s[slot] = o
        m_s[slot] = jnp.broadcast_to(top, (lanes, 128))
        l_s[slot] = jnp.broadcast_to(tot, (lanes, 128))

        @pl.when(s >= nb)
        def _():
            mc, lc = [], []
            for r in range(2 * rows):
                g_r = gid[t * (2 * rows) + r]
                src = jnp.where(g_r == g_low, nb, jnp.maximum(g_r - 1, 0))
                a, b = r * per_kv, (r + 1) * per_kv
                sendb[t, a:b, :] = acc_s[src, a:b, :].astype(BF16)
                mc.append(m_s[src, a:b, :])
                lc.append(l_s[src, a:b, :])
            mrow = jnp.sum(jnp.where(prow == plane, jnp.concatenate(mc, axis=0), 0.0), axis=0, keepdims=True)
            lrow = jnp.sum(jnp.where(prow == plane, jnp.concatenate(lc, axis=0), 0.0), axis=0, keepdims=True)
            high = lrow.astype(BF16).astype(F32)
            sub = lax.broadcasted_iota(jnp.int32, (16, 128), 0)
            block = jnp.where(sub == 0, mrow, jnp.where(sub == 1, high, jnp.where(sub == 2, lrow - high, 0.0)))
            sendb[t, lanes:lanes + 16, :] = block.astype(BF16)

            @pl.when(t != chip)
            def _():
                o_copy(t, chip).start()

        return carry

    lax.fori_loop(0, nb + chips, step, jnp.int32(0))
    own = pltpu.make_async_copy(sendb.at[chip], recvb.at[chip], loc.at[5])
    own.start()

    x_copy().wait_recv()
    own.wait()

    @pl.loop(1, chips)
    def _(j):
        o_copy(chip, (chip + j) % chips).wait_recv()

    ms, ls = [], []
    for i in range(chips):
        block = recvb[i, lanes:lanes + 16, :].astype(F32)
        ms.append(block[0:1])
        ls.append(block[1:2] + block[2:3])
    for block in (sfx[core, half:half + 8, :], sfx_in[half:half + 8, :]):
        ms.append(block[0:1])
        ls.append(block[1:2])
    peak = functools.reduce(jnp.maximum, ms)
    ws = [jnp.exp2(m - peak) for m in ms]
    inv = 1.0 / sum(a * b for a, b in zip(ws, ls))
    coef[...] = jnp.zeros_like(coef)
    for i, a in enumerate(ws):
        coef[i:i + 1, :] = a * inv
    ct = coef[...].T
    acc = jnp.zeros((lanes, hd), F32)
    for i in range(chips):
        acc += ct[:, i:i + 1] * recvb[i, :lanes, :].astype(F32)
    fin[...] = acc
    mo = pl.ds(pl.multiple_of(core * half, half), half)
    so = pl.ds(pl.multiple_of(other * half, half), half)
    smc[0] = jnp.where(core == 0, ct[:half, chips:chips + 1], ct[half:, chips:chips + 1]) * sfx[core, :half, :]
    smc[1] = jnp.where(core == 0, ct[half:, chips + 1:chips + 2], ct[:half, chips + 1:chips + 2]) * sfx_in[:half, :]
    fin[mo, :] += smc[0]
    fin[so, :] += smc[1]
    for h in range(per_kv):
        attn_all[chip, :, h * hd:(h + 1) * hd] = fin[pl.ds(h, 2 * rows, stride=per_kv), :].astype(BF16)

    def a_copy(dst_chip, src_chip):
        return to_page(
            attn_all.at[src_chip], attn_all.at[src_chip], a_ss.at[dst_chip], a_rs.at[src_chip], dst_chip * 2 + core)

    @pl.loop(1, chips)
    def _(j):
        a_copy((chip + j) % chips, chip).start()

    loads[3].wait()
    w_copy().wait_recv()
    zrows = out.shape[0]
    pin[z * 2 + core] = jnp.zeros(pin.shape[1:], BF16)

    @pl.loop(1, chips)
    def _(j):
        a_copy(chip, (chip + j) % chips).wait_recv()

    for i in range(chips // 2):
        pair = jnp.concatenate([attn_all[2 * i].astype(F32), attn_all[2 * i + 1].astype(F32)], axis=0)
        a_mat[i * 4 * rows:(i + 1) * 4 * rows, :] = pair.astype(BF16)

    def p_copy(dst_z, dst_core, src_z, src_core):
        return pltpu.make_async_remote_copy(
            src_ref=part.at[dst_z * 2 + dst_core], dst_ref=pin.at[src_z * 2 + src_core],
            send_sem=p_ss.at[dst_z * 2 + dst_core], recv_sem=p_rs.at[src_z * 2 + src_core],
            device_id={"kvh": dst_z, "page": chip * 2 + dst_core}, device_id_type=MESH)

    y = jnp.dot(a_mat[...], wr[...], preferred_element_type=F32)
    for k in range(zs):
        part[k * 2 + other] = y[k * zrows:(k + 1) * zrows].astype(BF16)

    @pl.loop(0, zs)
    def _(j):
        p_copy((z + j) % zs, other, z, core).start()

    y = jnp.dot(a_mat[...], wl[...], preferred_element_type=F32)
    pf[...] = y
    for k in range(zs):
        part[k * 2 + core] = y[k * zrows:(k + 1) * zrows].astype(BF16)

    @pl.loop(1, zs)
    def _(j):
        p_copy((z + j) % zs, core, z, core).start()

    @pl.loop(0, zs)
    def _(j):
        p_copy(z, core, (z + j) % zs, other).wait_recv()

    @pl.loop(1, zs)
    def _(j):
        p_copy(z, core, (z + j) % zs, core).wait_recv()

    total = pf[pl.ds(pl.multiple_of(z * zrows, zrows), zrows), :]
    for i in range(2 * zs):
        total += pin[i].astype(F32)
    out[...] = total.astype(BF16)

    @pl.loop(1, pages)
    def _(j):
        q_copy((me + j) % pages, me).wait_send()

    for g in range(groups):
        for i in range(2):
            kv_copy(g, i).wait_send()
    w_copy().wait_send()
    x_copy().wait_send()

    @pl.loop(1, chips)
    def _(j):
        o_copy((chip + j) % chips, chip).wait_send()
        a_copy((chip + j) % chips, chip).wait_send()

    @pl.loop(0, zs)
    def _(j):
        p_copy((z + j) % zs, other, z, core).wait_send()

    @pl.loop(1, zs)
    def _(j):
        p_copy((z + j) % zs, core, z, core).wait_send()


def on_device(pages, zs, queries, gid, slen, tab, pk, pv, sk, sv, w):
    rows, heads, hd = queries.shape
    groups, tokens, kvs = pk.shape[:3]
    per_kv = heads // kvs
    pool, plen = sk.shape[:2]
    sufp = tab.shape[1]
    chips = pages // 2
    lanes = 2 * rows * per_kv
    half = rows * per_kv
    feats, cols = w.shape
    fh = feats // 2
    zrows = rows * pages // zs
    pk = pk.reshape(groups, tokens * kvs, hd)
    pv = pv.reshape(groups, tokens * kvs, hd)
    sk = sk.reshape(pool, plen * kvs, hd)
    sv = sv.reshape(pool, plen * kvs, hd)
    V, D = pltpu.VMEM, pltpu.SemaphoreType.DMA
    smem = pl.BlockSpec(memory_space=pltpu.SMEM)
    anym = pl.BlockSpec(memory_space=pl.ANY)
    scratch = [
        V((rows, heads, hd), BF16), V((chips, 2, rows, per_kv, hd), BF16),
        V((groups, 2 * tokens, hd), BF16), V((groups, 2 * tokens, hd), BF16), V((2 * tokens, hd), F32),
        V((groups, 2, tokens, hd), BF16), V((groups, 2, tokens, hd), BF16),
        V((groups, tokens, hd), BF16), V((groups, tokens, hd), BF16),
        V((pool, plen * kvs, hd), BF16), V((pool, plen * kvs, hd), BF16),
        V((fh, cols), BF16), V((fh, cols), BF16), V((lanes, 2 * tokens), F32),
        V((groups, lanes, hd), F32), V((groups, lanes, 128), F32), V((groups, lanes, 128), F32),
        V((chips, lanes + 16, hd), BF16), V((chips, lanes + 16, hd), BF16),
        V((2, half + 8, hd), F32), V((half + 8, hd), F32), V((2, half, 128), F32), V((2, half, 128), F32),
        V((128, 128), F32), V((lanes, hd), F32), V((chips, 2 * rows, fh), BF16), V((rows * pages, fh), BF16),
        V((rows * pages, cols), F32), V((2 * zs, zrows, cols), BF16), V((2 * zs, zrows, cols), BF16),
        D((6 + 2 * groups,)), D((pages,)), D((pages,)), D((2 * groups,)), D((2 * groups,)), D, D, D, D,
        D((chips,)), D((chips,)), D((chips,)), D((chips,)), D((2 * zs,)), D((2 * zs,)),
    ]
    dims = (rows, per_kv, hd, tokens, groups, sufp)
    return pl.pallas_call(
        functools.partial(kernel, pages, zs, dims),
        out_shape=jax.ShapeDtypeStruct((zrows, cols), BF16),
        in_specs=[smem] * 3 + [anym] * 6,
        out_specs=pl.BlockSpec(memory_space=pltpu.VMEM),
        scratch_shapes=scratch,
        compiler_params=pltpu.CompilerParams(
            collective_id=0, has_side_effects=True, vmem_limit_bytes=56 * 1024 * 1024),
    )(gid, slen, tab, queries, pk, pv, sk, sv, w)


def solution(mesh):
    placed = (
        P("page", "kvh", None), P(), P("page"), P("page", None),
        P(None, "page", "kvh", None), P(None, "page", "kvh", None),
        P("page", None, "kvh", None), P("page", None, "kvh", None), P("kvh", "page"),
    )
    return jax.shard_map(
        functools.partial(on_device, mesh.shape["page"], mesh.shape["kvh"]),
        mesh=mesh, in_specs=placed, out_specs=P("kvh", "page"), check_vma=False)
```

```python
import functools
import math

import jax
import jax.numpy as jnp
from jax import lax
from jax.experimental import pallas as pl
from jax.experimental.pallas import tpu as pltpu
from jax.sharding import PartitionSpec as P

MESH = pl.DeviceIdType.MESH
F32 = jnp.float32
BF16 = jnp.bfloat16
LOW = -1e30


def nt_dot(a, b):
    return lax.dot_general(a, b, (((1,), (1,)), ((), ())), preferred_element_type=F32)


def kernel(
    pages, zs, sides, dims,
    gid, slen, tab, q_in, pk, pv, sk, sv, w_in, out,
    qv, q_all, kraw, vraw, stage, kd, vd, kr, vr, skv, svv, wl, wr, s_ref,
    acc_s, m_s, l_s, sendb, recvb, sfx, sfx_in, smc, slc, coef, fin, attn_all, a_mat, pf, part, pin,
    loc, q_ss, q_rs, kv_ss, kv_rs, w_ss, w_rs, x_ss, x_rs, o_ss, o_rs, a_ss, a_rs, p_ss, p_rs,
):
    rows, per_kv, hd, tokens, groups, sufp = dims
    chips = pages // 2
    lanes = 2 * rows * per_kv
    c2 = hd ** (-0.5) * math.log2(math.e)
    me = lax.axis_index("page")
    z = lax.axis_index("kvh")
    chip = me // 2
    core = me % 2
    other = 1 - core
    sib = chip * 2 + other
    far = [sorted(range(n), key=lambda d: -min(d, n - d)) for n in sides]

    def peer(j):
        def pick(order, i):
            d = jnp.int32(order[0])
            for k, v in enumerate(order[1:]):
                d = jnp.where(i == k + 1, v, d)
            return d

        x = (chip // sides[1] + pick(far[0], j // sides[1])) % sides[0]
        y = (chip % sides[1] + pick(far[1], j % sides[1])) % sides[1]
        return x * sides[1] + y

    def to_page(src, dst, ss, rs, page):
        return pltpu.make_async_remote_copy(
            src_ref=src, dst_ref=dst, send_sem=ss, recv_sem=rs,
            device_id={"page": page}, device_id_type=MESH)

    loads = [
        pltpu.make_async_copy(q_in, qv, loc.at[0]),
        pltpu.make_async_copy(sk, skv, loc.at[1]),
        pltpu.make_async_copy(sv, svv, loc.at[2]),
        pltpu.make_async_copy(w_in.at[pl.ds(core * wl.shape[0], wl.shape[0])], wl, loc.at[3]),
        pltpu.make_async_copy(q_in.at[:, pl.ds(core * per_kv, per_kv)], q_all.at[chip, core], loc.at[4]),
    ]
    kvl = []
    for g in range(groups):
        kvl.append(pltpu.make_async_copy(pk.at[g], kraw.at[g], loc.at[6 + 2 * g]))
        kvl.append(pltpu.make_async_copy(pv.at[g], vraw.at[g], loc.at[7 + 2 * g]))
    for copy in [loads[0], loads[4]] + kvl + loads[1:4]:
        copy.start()

    bar = pltpu.get_barrier_semaphore()

    @pl.loop(1, pages)
    def _(j):
        pl.semaphore_signal(bar, inc=1, device_id={"page": (me + j) % pages}, device_id_type=MESH)

    @pl.loop(1, zs)
    def _(j):
        for cc in range(2):
            pl.semaphore_signal(
                bar, inc=1, device_id={"kvh": (z + j) % zs, "page": chip * 2 + cc}, device_id_type=MESH)

    pl.semaphore_wait(bar, pages - 1 + 2 * (zs - 1))

    def q_copy(page, src_page):
        kv = page % 2
        return to_page(
            q_in.at[:, pl.ds(kv * per_kv, per_kv)], q_all.at[src_page // 2, src_page % 2],
            q_ss.at[page], q_rs.at[src_page], page)

    @pl.loop(0, pages - 1)
    def _(j):
        q_copy(jnp.where(j == pages - 2, sib, peer(j // 2) * 2 + j % 2), me).start()

    def count(r, c):
        g = gid[r]
        return tuple(c[e] + (g <= e).astype(jnp.int32) for e in range(groups - 1))

    first = lax.fori_loop(0, rows * pages, count, (jnp.int32(0),) * (groups - 1))
    btile = [jnp.minimum(f // (2 * rows), chips - 1) for f in first]

    def kv_copy(g, i):
        return to_page((kd, vd)[i].at[g, other], (kr, vr)[i].at[g], kv_ss.at[2 * g + i], kv_rs.at[2 * g + i], sib)

    for g in range(groups):
        for i in range(2):
            kvl[2 * g + i].wait()
            stage[...] = (kraw, vraw)[i][g].astype(F32)
            for kv in range(2):
                (kd, vd)[i][g, kv] = stage[pl.ds(kv, tokens, stride=2), :].astype(BF16)
            kv_copy(g, i).start()

    def w_copy():
        return to_page(w_in.at[pl.ds(other * wl.shape[0], wl.shape[0])], wr, w_ss, w_rs, sib)

    w_copy().start()

    span = sufp * skv.shape[1]
    both = 2 * per_kv
    col = lax.broadcasted_iota(jnp.int32, (both, span), 1)
    row = lax.broadcasted_iota(jnp.int32, (both, span), 0)
    mine = (col % 2) == (row // per_kv)
    token = col // 2
    for copy in loads[:3]:
        copy.wait()
    for r in range(rows):
        pgs = [tab[r, j] % skv.shape[0] for j in range(sufp)]
        keys = jnp.concatenate([skv[pg] for pg in pgs], axis=0)
        vals = jnp.concatenate([svv[pg] for pg in pgs], axis=0)
        live = mine & (token < slen[r])
        s = jnp.where(live, nt_dot(qv[r], keys) * c2, LOW)
        top = jnp.max(s, axis=1, keepdims=True)
        p = jnp.where(live, jnp.exp2(s - top), 0.0)
        tot = jnp.sum(p, axis=1, keepdims=True)
        o = jnp.dot(p.astype(BF16), vals, preferred_element_type=F32)
        for kv in range(2):
            a, b = kv * per_kv, (kv + 1) * per_kv
            sfx[kv, r * per_kv:(r + 1) * per_kv, :] = o[a:b]
            smc[kv, r * per_kv:(r + 1) * per_kv, :] = jnp.broadcast_to(top[a:b], (per_kv, 128))
            slc[kv, r * per_kv:(r + 1) * per_kv, :] = jnp.broadcast_to(tot[a:b], (per_kv, 128))
    half = rows * per_kv
    hrow = lax.broadcasted_iota(jnp.int32, (half, 128), 0) + core * half
    hlane = lax.broadcasted_iota(jnp.int32, (half, 128), 1)
    sub8 = lax.broadcasted_iota(jnp.int32, (8, 128), 0)
    lane8 = lax.broadcasted_iota(jnp.int32, (8, 128), 1)
    held = (lane8 // half) == core
    for kv in range(2):
        mrow = jnp.sum(jnp.where(hrow == hlane, smc[kv], 0.0), axis=0, keepdims=True)
        lrow = jnp.sum(jnp.where(hrow == hlane, slc[kv], 0.0), axis=0, keepdims=True)
        block = jnp.where(sub8 == 0, mrow, jnp.where(sub8 == 1, lrow, 0.0))
        sfx[kv, half:half + 8, :] = jnp.where(held, block, jnp.where(sub8 == 0, LOW, 0.0))

    def x_copy():
        return to_page(sfx.at[other], sfx_in, x_ss, x_rs, sib)

    x_copy().start()

    loads[4].wait()

    @pl.loop(1, pages)
    def _(j):
        q_copy(me, (me + j) % pages).wait_recv()

    for g in range(groups):
        for i in range(2):
            kv_copy(g, i).wait_recv()

    def o_copy(dst_chip, src_chip):
        return to_page(sendb.at[dst_chip], recvb.at[src_chip], o_ss.at[dst_chip], o_rs.at[src_chip], dst_chip * 2 + core)

    prow = lax.broadcasted_iota(jnp.int32, (lanes, 128), 0)
    plane = lax.broadcasted_iota(jnp.int32, (lanes, 128), 1)
    nb = groups - 1

    def tile_of(k):
        t = peer(k)
        return t, gid[t * (2 * rows)]

    def columns(f, x):
        return functools.reduce(f, [x[:, i * 128:(i + 1) * 128] for i in range(tokens // 128)] if tokens > 128 else [x])

    def advance(now, then, slot, top_in):
        if now is not None:
            top = (jnp.max(top_in, axis=1, keepdims=True) * c2).astype(BF16).astype(F32)
        if then is not None:
            q = q_all[then[0]].reshape(lanes, hd)
        o, tot, top_out = None, None, None
        for i in range(2):
            part_of = slice(i * tokens, (i + 1) * tokens)
            if then is not None:
                x = nt_dot(q, kr[then[1]] if i else kd[then[1], core])
                s_ref[1 - slot, :, part_of] = x
                m = columns(jnp.maximum, x)
                top_out = m if i == 0 else jnp.maximum(top_out, m)
            if now is not None:
                p = jnp.exp2(s_ref[slot, :, part_of] * c2 - top)
                l = columns(jnp.add, p)
                tot = l if i == 0 else tot + l
                d = jnp.dot(p.astype(BF16), vr[now] if i else vd[now, core], preferred_element_type=F32)
                o = d if i == 0 else o + d
        if now is None:
            return top_out
        return top_out, o, top, jnp.sum(tot, axis=1, keepdims=True)

    def keep(at, o, top, tot):
        acc_s[at] = o
        m_s[at] = jnp.broadcast_to(top, (lanes, 128))
        l_s[at] = jnp.broadcast_to(tot, (lanes, 128))

    def finish(k):
        t, g_low = tile_of(k)
        mc, lc = [], []
        for r in range(2 * rows):
            g_r = gid[t * (2 * rows) + r]
            src = jnp.where(g_r == g_low, nb, jnp.maximum(g_r - 1, 0))
            a, b = r * per_kv, (r + 1) * per_kv
            sendb[t, a:b, :] = acc_s[src, a:b, :].astype(BF16)
            mc.append(m_s[src, a:b, :])
            lc.append(l_s[src, a:b, :])
        mrow = jnp.sum(jnp.where(prow == plane, jnp.concatenate(mc, axis=0), 0.0), axis=0, keepdims=True)
        lrow = jnp.sum(jnp.where(prow == plane, jnp.concatenate(lc, axis=0), 0.0), axis=0, keepdims=True)
        high = lrow.astype(BF16).astype(F32)
        sub = lax.broadcasted_iota(jnp.int32, (16, 128), 0)
        block = jnp.where(sub == 0, mrow, jnp.where(sub == 1, high, jnp.where(sub == 2, lrow - high, 0.0)))
        sendb[t, lanes:lanes + 16, :] = block.astype(BF16)

    top = advance(None, (btile[0], 1), 1, None)
    for e in range(nb):
        then = (btile[e + 1], e + 2) if e + 1 < nb else tile_of(0)
        top, *res = advance(e + 1, then, e % 2, top)
        keep(e, *res)
    base = nb % 2

    def one(k, slot, top, last=False):
        t, g = tile_of(k)
        top, *res = advance(g, None if last else tile_of(k + 1), slot, top)
        keep(nb, *res)
        finish(k)
        if not last:
            o_copy(t, chip).start()
        return top

    def pair(i, top):
        return one(2 * i + 1, 1 - base, one(2 * i, base, top))

    top = lax.fori_loop(0, chips // 2 - 1, pair, top)
    top = one(chips - 2, base, top)
    one(chips - 1, 1 - base, top, last=True)
    own = pltpu.make_async_copy(sendb.at[chip], recvb.at[chip], loc.at[5])
    own.start()

    x_copy().wait_recv()
    own.wait()

    @pl.loop(1, chips)
    def _(j):
        o_copy(chip, (chip + j) % chips).wait_recv()

    ms, ls = [], []
    for i in range(chips):
        block = recvb[i, lanes:lanes + 16, :].astype(F32)
        ms.append(block[0:1])
        ls.append(block[1:2] + block[2:3])
    for block in (sfx[core, half:half + 8, :], sfx_in[half:half + 8, :]):
        ms.append(block[0:1])
        ls.append(block[1:2])
    peak = functools.reduce(jnp.maximum, ms)
    ws = [jnp.exp2(m - peak) for m in ms]
    inv = 1.0 / sum(a * b for a, b in zip(ws, ls))
    coef[...] = jnp.zeros_like(coef)
    for i, a in enumerate(ws):
        coef[i:i + 1, :] = a * inv
    ct = coef[...].T
    acc = jnp.zeros((lanes, hd), F32)
    for i in range(chips):
        acc += ct[:, i:i + 1] * recvb[i, :lanes, :].astype(F32)
    fin[...] = acc
    mo = pl.ds(pl.multiple_of(core * half, half), half)
    so = pl.ds(pl.multiple_of(other * half, half), half)
    smc[0] = jnp.where(core == 0, ct[:half, chips:chips + 1], ct[half:, chips:chips + 1]) * sfx[core, :half, :]
    smc[1] = jnp.where(core == 0, ct[half:, chips + 1:chips + 2], ct[:half, chips + 1:chips + 2]) * sfx_in[:half, :]
    fin[mo, :] += smc[0]
    fin[so, :] += smc[1]
    for h in range(per_kv):
        attn_all[chip, :, h * hd:(h + 1) * hd] = fin[pl.ds(h, 2 * rows, stride=per_kv), :].astype(BF16)

    def a_copy(dst_chip, src_chip):
        return to_page(
            attn_all.at[src_chip], attn_all.at[src_chip], a_ss.at[dst_chip], a_rs.at[src_chip], dst_chip * 2 + core)

    @pl.loop(0, chips - 1)
    def _(j):
        a_copy(peer(j), chip).start()

    loads[3].wait()
    w_copy().wait_recv()
    zrows = out.shape[0]
    pin[z * 2 + core] = jnp.zeros(pin.shape[1:], BF16)

    @pl.loop(1, chips)
    def _(j):
        a_copy(chip, (chip + j) % chips).wait_recv()

    for i in range(chips // 2):
        pair = jnp.concatenate([attn_all[2 * i].astype(F32), attn_all[2 * i + 1].astype(F32)], axis=0)
        a_mat[i * 4 * rows:(i + 1) * 4 * rows, :] = pair.astype(BF16)

    def p_copy(dst_z, dst_core, src_z, src_core):
        return pltpu.make_async_remote_copy(
            src_ref=part.at[dst_z * 2 + dst_core], dst_ref=pin.at[src_z * 2 + src_core],
            send_sem=p_ss.at[dst_z * 2 + dst_core], recv_sem=p_rs.at[src_z * 2 + src_core],
            device_id={"kvh": dst_z, "page": chip * 2 + dst_core}, device_id_type=MESH)

    y = jnp.dot(a_mat[...], wr[...], preferred_element_type=F32)
    for k in range(zs):
        part[k * 2 + other] = y[k * zrows:(k + 1) * zrows].astype(BF16)

    @pl.loop(0, zs)
    def _(j):
        p_copy((z + j) % zs, other, z, core).start()

    y = jnp.dot(a_mat[...], wl[...], preferred_element_type=F32)
    pf[...] = y
    for k in range(zs):
        part[k * 2 + core] = y[k * zrows:(k + 1) * zrows].astype(BF16)

    @pl.loop(1, zs)
    def _(j):
        p_copy((z + j) % zs, core, z, core).start()

    @pl.loop(0, zs)
    def _(j):
        p_copy(z, core, (z + j) % zs, other).wait_recv()

    @pl.loop(1, zs)
    def _(j):
        p_copy(z, core, (z + j) % zs, core).wait_recv()

    total = pf[pl.ds(pl.multiple_of(z * zrows, zrows), zrows), :]
    for i in range(2 * zs):
        total += pin[i].astype(F32)
    out[...] = total.astype(BF16)

    @pl.loop(1, pages)
    def _(j):
        q_copy((me + j) % pages, me).wait_send()

    for g in range(groups):
        for i in range(2):
            kv_copy(g, i).wait_send()
    w_copy().wait_send()
    x_copy().wait_send()

    @pl.loop(1, chips)
    def _(j):
        o_copy((chip + j) % chips, chip).wait_send()
        a_copy((chip + j) % chips, chip).wait_send()

    @pl.loop(0, zs)
    def _(j):
        p_copy((z + j) % zs, other, z, core).wait_send()

    @pl.loop(1, zs)
    def _(j):
        p_copy((z + j) % zs, core, z, core).wait_send()


def on_device(pages, zs, queries, gid, slen, tab, pk, pv, sk, sv, w):
    rows, heads, hd = queries.shape
    groups, tokens, kvs = pk.shape[:3]
    per_kv = heads // kvs
    pool, plen = sk.shape[:2]
    sufp = tab.shape[1]
    chips = pages // 2
    side = math.isqrt(chips)
    side = side if side * side == chips else 1
    lanes = 2 * rows * per_kv
    half = rows * per_kv
    feats, cols = w.shape
    fh = feats // 2
    zrows = rows * pages // zs
    pk = pk.reshape(groups, tokens * kvs, hd)
    pv = pv.reshape(groups, tokens * kvs, hd)
    sk = sk.reshape(pool, plen * kvs, hd)
    sv = sv.reshape(pool, plen * kvs, hd)
    V, D = pltpu.VMEM, pltpu.SemaphoreType.DMA
    smem = pl.BlockSpec(memory_space=pltpu.SMEM)
    anym = pl.BlockSpec(memory_space=pl.ANY)
    scratch = [
        V((rows, heads, hd), BF16), V((chips, 2, rows, per_kv, hd), BF16),
        V((groups, 2 * tokens, hd), BF16), V((groups, 2 * tokens, hd), BF16), V((2 * tokens, hd), F32),
        V((groups, 2, tokens, hd), BF16), V((groups, 2, tokens, hd), BF16),
        V((groups, tokens, hd), BF16), V((groups, tokens, hd), BF16),
        V((pool, plen * kvs, hd), BF16), V((pool, plen * kvs, hd), BF16),
        V((fh, cols), BF16), V((fh, cols), BF16), V((2, lanes, 2 * tokens), F32),
        V((groups, lanes, hd), F32), V((groups, lanes, 128), F32), V((groups, lanes, 128), F32),
        V((chips, lanes + 16, hd), BF16), V((chips, lanes + 16, hd), BF16),
        V((2, half + 8, hd), F32), V((half + 8, hd), F32), V((2, half, 128), F32), V((2, half, 128), F32),
        V((128, 128), F32), V((lanes, hd), F32), V((chips, 2 * rows, fh), BF16), V((rows * pages, fh), BF16),
        V((rows * pages, cols), F32), V((2 * zs, zrows, cols), BF16), V((2 * zs, zrows, cols), BF16),
        D((6 + 2 * groups,)), D((pages,)), D((pages,)), D((2 * groups,)), D((2 * groups,)), D, D, D, D,
        D((chips,)), D((chips,)), D((chips,)), D((chips,)), D((2 * zs,)), D((2 * zs,)),
    ]
    dims = (rows, per_kv, hd, tokens, groups, sufp)
    return pl.pallas_call(
        functools.partial(kernel, pages, zs, (side, chips // side), dims),
        out_shape=jax.ShapeDtypeStruct((zrows, cols), BF16),
        in_specs=[smem] * 3 + [anym] * 6,
        out_specs=pl.BlockSpec(memory_space=pltpu.VMEM),
        scratch_shapes=scratch,
        compiler_params=pltpu.CompilerParams(
            collective_id=0, has_side_effects=True, vmem_limit_bytes=56 * 1024 * 1024),
    )(gid, slen, tab, queries, pk, pv, sk, sv, w)


def solution(mesh):
    placed = (
        P("page", "kvh", None), P(), P("page"), P("page", None),
        P(None, "page", "kvh", None), P(None, "page", "kvh", None),
        P("page", None, "kvh", None), P("page", None, "kvh", None), P("kvh", "page"),
    )
    return jax.shard_map(
        functools.partial(on_device, mesh.shape["page"], mesh.shape["kvh"]),
        mesh=mesh, in_specs=placed, out_specs=P("kvh", "page"), check_vma=False)
```

```python
import functools
import math

import jax
import jax.numpy as jnp
from jax import lax
from jax.experimental import pallas as pl
from jax.experimental.pallas import tpu as pltpu
from jax.sharding import PartitionSpec as P

MESH = pl.DeviceIdType.MESH
F32 = jnp.float32
BF16 = jnp.bfloat16
LOW = -1e30


def nt_dot(a, b):
    return lax.dot_general(a, b, (((1,), (1,)), ((), ())), preferred_element_type=F32)


def kernel(
    pages, zs, sides, dims,
    gid, slen, tab, q_in, pk, pv, sk, sv, w_in, out,
    qv, q_all, kraw, vraw, stage, kd, vd, kr, vr, skv, svv, wl, wr, s_ref,
    acc_s, m_s, l_s, sendb, recvb, own_part, sfx, sfx_in, smc, slc, coef, fin, attn_all, pf, part, pin,
    loc, q_ss, q_rs, kv_ss, kv_rs, w_ss, w_rs, x_ss, x_rs, o_ss, o_rs, a_ss, a_rs, p_ss, p_rs,
):
    rows, per_kv, hd, tokens, groups, sufp = dims
    chips = pages // 2
    lanes = 2 * rows * per_kv
    c2 = hd ** (-0.5) * math.log2(math.e)
    me = lax.axis_index("page")
    z = lax.axis_index("kvh")
    chip = me // 2
    core = me % 2
    other = 1 - core
    sib = chip * 2 + other

    offsets = [(i, j) for i in range(sides[0]) for j in range(sides[1])]
    far_first = sorted(offsets, key=lambda d: -sum(min(v, n - v) for v, n in zip(d, sides)))
    n1 = chips // 2

    def pick(table, i):
        v = jnp.int32(table[0])
        for k in range(1, len(table)):
            v = jnp.where(i == k, table[k], v)
        return v

    def at_offset(table, k):
        x = (chip // sides[1] + pick([d[0] for d in table], k)) % sides[0]
        y = (chip % sides[1] + pick([d[1] for d in table], k)) % sides[1]
        return x * sides[1] + y

    def peer(j):
        return at_offset(far_first, j)

    def to_page(src, dst, ss, rs, page):
        return pltpu.make_async_remote_copy(
            src_ref=src, dst_ref=dst, send_sem=ss, recv_sem=rs,
            device_id={"page": page}, device_id_type=MESH)

    loads = [
        pltpu.make_async_copy(q_in, qv, loc.at[0]),
        pltpu.make_async_copy(sk, skv, loc.at[1]),
        pltpu.make_async_copy(sv, svv, loc.at[2]),
        pltpu.make_async_copy(w_in.at[pl.ds(core * wl.shape[0], wl.shape[0])], wl, loc.at[3]),
        pltpu.make_async_copy(q_in.at[:, pl.ds(core * per_kv, per_kv)], q_all.at[chip, core], loc.at[4]),
    ]
    kvl = []
    for g in range(groups):
        kvl.append(pltpu.make_async_copy(pk.at[g], kraw.at[g], loc.at[6 + 2 * g]))
        kvl.append(pltpu.make_async_copy(pv.at[g], vraw.at[g], loc.at[7 + 2 * g]))
    for copy in [loads[0], loads[4]] + kvl + loads[1:4]:
        copy.start()

    bar = pltpu.get_barrier_semaphore()

    @pl.loop(1, pages)
    def _(j):
        pl.semaphore_signal(bar, inc=1, device_id={"page": (me + j) % pages}, device_id_type=MESH)

    @pl.loop(1, zs)
    def _(j):
        for cc in range(2):
            pl.semaphore_signal(
                bar, inc=1, device_id={"kvh": (z + j) % zs, "page": chip * 2 + cc}, device_id_type=MESH)

    def kv_copy(g, i):
        return to_page((kd, vd)[i].at[g, other], (kr, vr)[i].at[g], kv_ss.at[2 * g + i], kv_rs.at[2 * g + i], sib)

    for g in range(groups):
        for i in range(2):
            kvl[2 * g + i].wait()
            stage[...] = (kraw, vraw)[i][g].astype(F32)
            for kv in range(2):
                (kd, vd)[i][g, kv] = stage[pl.ds(kv, tokens, stride=2), :].astype(BF16)

    pl.semaphore_wait(bar, pages - 1 + 2 * (zs - 1))

    def q_copy(page, src_page):
        kv = page % 2
        return to_page(
            q_in.at[:, pl.ds(kv * per_kv, per_kv)], q_all.at[src_page // 2, src_page % 2],
            q_ss.at[page], q_rs.at[src_page], page)

    @pl.loop(0, pages - 1)
    def _(j):
        q_copy(jnp.where(j == pages - 2, sib, peer(j // 2) * 2 + j % 2), me).start()

    def count(r, c):
        g = gid[r]
        return tuple(c[e] + (g <= e).astype(jnp.int32) for e in range(groups - 1))

    first = lax.fori_loop(0, rows * pages, count, (jnp.int32(0),) * (groups - 1))
    btile = [jnp.minimum(f // (2 * rows), chips - 1) for f in first]

    for g in range(groups):
        for i in range(2):
            kv_copy(g, i).start()

    def w_copy():
        return to_page(w_in.at[pl.ds(other * wl.shape[0], wl.shape[0])], wr, w_ss, w_rs, sib)

    w_copy().start()

    span = sufp * skv.shape[1]
    both = 2 * per_kv
    col = lax.broadcasted_iota(jnp.int32, (both, span), 1)
    row = lax.broadcasted_iota(jnp.int32, (both, span), 0)
    mine = (col % 2) == (row // per_kv)
    token = col // 2
    for copy in loads[:3]:
        copy.wait()
    for r in range(rows):
        pgs = [tab[r, j] % skv.shape[0] for j in range(sufp)]
        keys = jnp.concatenate([skv[pg] for pg in pgs], axis=0)
        vals = jnp.concatenate([svv[pg] for pg in pgs], axis=0)
        live = mine & (token < slen[r])
        s = jnp.where(live, nt_dot(qv[r], keys) * c2, LOW)
        top = jnp.max(s, axis=1, keepdims=True)
        p = jnp.where(live, jnp.exp2(s - top), 0.0)
        tot = jnp.sum(p, axis=1, keepdims=True)
        o = jnp.dot(p.astype(BF16), vals, preferred_element_type=F32)
        for kv in range(2):
            a, b = kv * per_kv, (kv + 1) * per_kv
            sfx[kv, r * per_kv:(r + 1) * per_kv, :] = o[a:b]
            smc[kv, r * per_kv:(r + 1) * per_kv, :] = jnp.broadcast_to(top[a:b], (per_kv, 128))
            slc[kv, r * per_kv:(r + 1) * per_kv, :] = jnp.broadcast_to(tot[a:b], (per_kv, 128))
    half = rows * per_kv
    hrow = lax.broadcasted_iota(jnp.int32, (half, 128), 0) + core * half
    hlane = lax.broadcasted_iota(jnp.int32, (half, 128), 1)
    sub8 = lax.broadcasted_iota(jnp.int32, (8, 128), 0)
    lane8 = lax.broadcasted_iota(jnp.int32, (8, 128), 1)
    held = (lane8 // half) == core
    for kv in range(2):
        mrow = jnp.sum(jnp.where(hrow == hlane, smc[kv], 0.0), axis=0, keepdims=True)
        lrow = jnp.sum(jnp.where(hrow == hlane, slc[kv], 0.0), axis=0, keepdims=True)
        block = jnp.where(sub8 == 0, mrow, jnp.where(sub8 == 1, lrow, 0.0))
        sfx[kv, half:half + 8, :] = jnp.where(held, block, jnp.where(sub8 == 0, LOW, 0.0))

    def x_copy():
        return to_page(sfx.at[other], sfx_in, x_ss, x_rs, sib)

    x_copy().start()

    def o_copy(dst_chip, src_chip):
        return to_page(sendb.at[dst_chip], recvb.at[src_chip], o_ss.at[dst_chip], o_rs.at[src_chip], dst_chip * 2 + core)

    prow = lax.broadcasted_iota(jnp.int32, (lanes, 128), 0)
    plane = lax.broadcasted_iota(jnp.int32, (lanes, 128), 1)
    nb = groups - 1

    def tile_at(k):
        x = (chip // sides[1] + k // sides[1]) % sides[0]
        return x * sides[1] + (chip + k) % sides[1]

    def tile_of(k):
        t = tile_at(k)
        return t, gid[t * (2 * rows)]

    def q_wait(k):
        t = tile_at(k)
        for cc in range(2):
            q_copy(me, t * 2 + cc).wait_recv()

    def columns(f, x):
        return functools.reduce(f, [x[:, i * 128:(i + 1) * 128] for i in range(tokens // 128)] if tokens > 128 else [x])

    def advance(now, then, slot, top_in):
        if now is not None:
            top = (jnp.max(top_in, axis=1, keepdims=True) * c2).astype(BF16).astype(F32)
        if then is not None:
            q = q_all[then[0]].reshape(lanes, hd)
        o, tot, top_out = None, None, None
        for i in range(2):
            part_of = slice(i * tokens, (i + 1) * tokens)
            if then is not None:
                x = nt_dot(q, kr[then[1]] if i else kd[then[1], core])
                s_ref[1 - slot, :, part_of] = x
                m = columns(jnp.maximum, x)
                top_out = m if i == 0 else jnp.maximum(top_out, m)
            if now is not None:
                p = jnp.exp2(s_ref[slot, :, part_of] * c2 - top)
                l = columns(jnp.add, p)
                tot = l if i == 0 else tot + l
                d = jnp.dot(p.astype(BF16), vr[now] if i else vd[now, core], preferred_element_type=F32)
                o = d if i == 0 else o + d
        if now is None:
            return top_out
        return top_out, o, top, jnp.sum(tot, axis=1, keepdims=True)

    def keep(at, o, top, tot):
        acc_s[at] = o
        m_s[at] = jnp.broadcast_to(top, (lanes, 128))
        l_s[at] = jnp.broadcast_to(tot, (lanes, 128))

    def finish(k, slot, dst, at):
        t, g_low = tile_of(k)
        mc, lc = [], []
        for r in range(2 * rows):
            g_r = gid[t * (2 * rows) + r]
            src = jnp.where(g_r == g_low, slot, jnp.maximum(g_r - 1, 0))
            a, b = r * per_kv, (r + 1) * per_kv
            dst[at, a:b, :] = acc_s[src, a:b, :].astype(BF16)
            mc.append(m_s[src, a:b, :])
            lc.append(l_s[src, a:b, :])
        mrow = jnp.sum(jnp.where(prow == plane, jnp.concatenate(mc, axis=0), 0.0), axis=0, keepdims=True)
        lrow = jnp.sum(jnp.where(prow == plane, jnp.concatenate(lc, axis=0), 0.0), axis=0, keepdims=True)
        high = lrow.astype(BF16).astype(F32)
        sub = lax.broadcasted_iota(jnp.int32, (16, 128), 0)
        block = jnp.where(sub == 0, mrow, jnp.where(sub == 1, high, jnp.where(sub == 2, lrow - high, 0.0)))
        dst[at, lanes:lanes + 16, :] = block.astype(BF16)

    def send(k):
        o_copy(tile_at(k), chip).start()

    def run(first_k, count, side, top, body):
        def two(i, top):
            k = first_k + 2 * i
            return body(k + 1, 1 - side, body(k, side, top))

        pairs = (count - 1) // 2
        top = lax.fori_loop(0, pairs, two, top)
        for k in range(2 * pairs, count):
            top = body(first_k + k, side, top, k == count - 1)
            side = 1 - side
        return side, top

    loads[4].wait()
    q_copy(me, sib).wait_recv()
    for g in range(groups):
        for i in range(2):
            kv_copy(g, i).wait_recv()
    @pl.loop(1, chips)
    def _(j):
        q_wait(j)

    top = advance(None, tile_of(0), 1, None)

    def before(k, slot, top, last=False):
        if last:
            then = (btile[0], 1)
        else:
            then = tile_of(k + 1)
        top, *res = advance(tile_of(k)[1], then, slot, top)
        keep(nb + k, *res)
        return top

    slot, top = run(0, n1, 0, top, before)

    for e in range(nb):
        then = (btile[e + 1], e + 2) if e + 1 < nb else tile_of(n1)
        top, *res = advance(e + 1, then, slot, top)
        keep(e, *res)
        slot = 1 - slot

    @pl.loop(0, n1 - 1)
    def _(j):
        k = n1 - 1 - j
        finish(k, nb + k, sendb, tile_at(k))
        send(k)

    finish(0, nb, own_part, 0)

    def after(k, slot, top, last=False):
        top, *res = advance(tile_of(k)[1], None if last else tile_of(k + 1), slot, top)
        keep(nb, *res)
        finish(k, nb, sendb, tile_at(k))
        send(k)
        return top

    run(n1, chips - n1, slot, top, after)

    x_copy().wait_recv()

    @pl.loop(1, chips)
    def _(j):
        o_copy(chip, (chip + j) % chips).wait_recv()

    def partial(i, part_rows):
        return (recvb[(chip + i) % chips, part_rows, :] if i else own_part[0, part_rows, :]).astype(F32)

    ms, ls = [], []
    for i in range(chips):
        block = partial(i, slice(lanes, lanes + 16))
        ms.append(block[0:1])
        ls.append(block[1:2] + block[2:3])
    for block in (sfx[core, half:half + 8, :], sfx_in[half:half + 8, :]):
        ms.append(block[0:1])
        ls.append(block[1:2])
    peak = functools.reduce(jnp.maximum, ms)
    ws = [jnp.exp2(m - peak) for m in ms]
    inv = 1.0 / sum(a * b for a, b in zip(ws, ls))
    coef[...] = jnp.zeros_like(coef)
    for i, a in enumerate(ws):
        coef[i:i + 1, :] = a * inv
    ct = coef[...].T
    acc = jnp.zeros((lanes, hd), F32)
    for i in range(chips):
        acc += ct[:, i:i + 1] * partial(i, slice(0, lanes))
    fin[...] = acc
    mo = pl.ds(pl.multiple_of(core * half, half), half)
    so = pl.ds(pl.multiple_of(other * half, half), half)
    smc[0] = jnp.where(core == 0, ct[:half, chips:chips + 1], ct[half:, chips:chips + 1]) * sfx[core, :half, :]
    smc[1] = jnp.where(core == 0, ct[half:, chips + 1:chips + 2], ct[:half, chips + 1:chips + 2]) * sfx_in[:half, :]
    fin[mo, :] += smc[0]
    fin[so, :] += smc[1]
    for h in range(per_kv):
        attn_all[chip, :, h * hd:(h + 1) * hd] = fin[pl.ds(h, 2 * rows, stride=per_kv), :].astype(BF16)

    def a_copy(dst_chip, src_chip):
        return to_page(
            attn_all.at[src_chip], attn_all.at[src_chip], a_ss.at[dst_chip], a_rs.at[src_chip], dst_chip * 2 + core)

    @pl.loop(0, chips - 1)
    def _(j):
        a_copy(peer(j), chip).start()

    loads[3].wait()
    w_copy().wait_recv()
    zrows = out.shape[0]
    pin[z * 2 + core] = jnp.zeros(pin.shape[1:], BF16)

    def p_copy(dst_z, dst_core, src_z, src_core):
        return pltpu.make_async_remote_copy(
            src_ref=part.at[dst_z * 2 + dst_core], dst_ref=pin.at[src_z * 2 + src_core],
            send_sem=p_ss.at[dst_z * 2 + dst_core], recv_sem=p_rs.at[src_z * 2 + src_core],
            device_id={"kvh": dst_z, "page": chip * 2 + dst_core}, device_id_type=MESH)

    @pl.loop(1, chips)
    def _(j):
        a_copy(chip, (chip + j) % chips).wait_recv()

    got = [attn_all[i].astype(F32) for i in range(chips)]
    a = jnp.concatenate(got, axis=0).astype(BF16)
    y = jnp.dot(a, wr[...], preferred_element_type=F32)
    for k in range(zs):
        part[k * 2 + other] = y[k * zrows:(k + 1) * zrows].astype(BF16)

    @pl.loop(0, zs)
    def _(j):
        p_copy((z + j) % zs, other, z, core).start()

    y = jnp.dot(a, wl[...], preferred_element_type=F32)
    pf[...] = y
    for k in range(zs):
        part[k * 2 + core] = y[k * zrows:(k + 1) * zrows].astype(BF16)

    @pl.loop(1, zs)
    def _(j):
        p_copy((z + j) % zs, core, z, core).start()

    @pl.loop(0, zs)
    def _(j):
        p_copy(z, core, (z + j) % zs, other).wait_recv()

    @pl.loop(1, zs)
    def _(j):
        p_copy(z, core, (z + j) % zs, core).wait_recv()

    total = pf[pl.ds(pl.multiple_of(z * zrows, zrows), zrows), :]
    for i in range(2 * zs):
        total += pin[i].astype(F32)
    out[...] = total.astype(BF16)

    @pl.loop(1, pages)
    def _(j):
        q_copy((me + j) % pages, me).wait_send()

    for g in range(groups):
        for i in range(2):
            kv_copy(g, i).wait_send()
    w_copy().wait_send()
    x_copy().wait_send()

    @pl.loop(1, chips)
    def _(j):
        o_copy((chip + j) % chips, chip).wait_send()
        a_copy((chip + j) % chips, chip).wait_send()

    @pl.loop(0, zs)
    def _(j):
        p_copy((z + j) % zs, other, z, core).wait_send()

    @pl.loop(1, zs)
    def _(j):
        p_copy((z + j) % zs, core, z, core).wait_send()


def on_device(pages, zs, queries, gid, slen, tab, pk, pv, sk, sv, w):
    rows, heads, hd = queries.shape
    groups, tokens, kvs = pk.shape[:3]
    per_kv = heads // kvs
    pool, plen = sk.shape[:2]
    sufp = tab.shape[1]
    chips = pages // 2
    side = math.isqrt(chips)
    side = side if side * side == chips else 1
    lanes = 2 * rows * per_kv
    half = rows * per_kv
    kept = groups - 1 + chips // 2
    feats, cols = w.shape
    fh = feats // 2
    zrows = rows * pages // zs
    pk = pk.reshape(groups, tokens * kvs, hd)
    pv = pv.reshape(groups, tokens * kvs, hd)
    sk = sk.reshape(pool, plen * kvs, hd)
    sv = sv.reshape(pool, plen * kvs, hd)
    V, D = pltpu.VMEM, pltpu.SemaphoreType.DMA
    smem = pl.BlockSpec(memory_space=pltpu.SMEM)
    anym = pl.BlockSpec(memory_space=pl.ANY)
    scratch = [
        V((rows, heads, hd), BF16), V((chips, 2, rows, per_kv, hd), BF16),
        V((groups, 2 * tokens, hd), BF16), V((groups, 2 * tokens, hd), BF16), V((2 * tokens, hd), F32),
        V((groups, 2, tokens, hd), BF16), V((groups, 2, tokens, hd), BF16),
        V((groups, tokens, hd), BF16), V((groups, tokens, hd), BF16),
        V((pool, plen * kvs, hd), BF16), V((pool, plen * kvs, hd), BF16),
        V((fh, cols), BF16), V((fh, cols), BF16), V((2, lanes, 2 * tokens), F32),
        V((kept, lanes, hd), F32), V((kept, lanes, 128), F32), V((kept, lanes, 128), F32),
        V((chips, lanes + 16, hd), BF16), V((chips, lanes + 16, hd), BF16), V((1, lanes + 16, hd), BF16),
        V((2, half + 8, hd), F32), V((half + 8, hd), F32), V((2, half, 128), F32), V((2, half, 128), F32),
        V((128, 128), F32), V((lanes, hd), F32), V((chips, 2 * rows, fh), BF16),
        V((rows * pages, cols), F32), V((2 * zs, zrows, cols), BF16), V((2 * zs, zrows, cols), BF16),
        D((6 + 2 * groups,)), D((pages,)), D((pages,)), D((2 * groups,)), D((2 * groups,)), D, D, D, D,
        D((chips,)), D((chips,)), D((chips,)), D((chips,)), D((2 * zs,)), D((2 * zs,)),
    ]
    dims = (rows, per_kv, hd, tokens, groups, sufp)
    return pl.pallas_call(
        functools.partial(kernel, pages, zs, (side, chips // side), dims),
        out_shape=jax.ShapeDtypeStruct((zrows, cols), BF16),
        in_specs=[smem] * 3 + [anym] * 6,
        out_specs=pl.BlockSpec(memory_space=pltpu.VMEM),
        scratch_shapes=scratch,
        compiler_params=pltpu.CompilerParams(
            collective_id=0, has_side_effects=True, vmem_limit_bytes=56 * 1024 * 1024),
    )(gid, slen, tab, queries, pk, pv, sk, sv, w)


def solution(mesh):
    placed = (
        P("page", "kvh", None), P(), P("page"), P("page", None),
        P(None, "page", "kvh", None), P(None, "page", "kvh", None),
        P("page", None, "kvh", None), P("page", None, "kvh", None), P("kvh", "page"),
    )
    return jax.shard_map(
        functools.partial(on_device, mesh.shape["page"], mesh.shape["kvh"]),
        mesh=mesh, in_specs=placed, out_specs=P("kvh", "page"), check_vma=False)
```

```python
import functools
import math

import jax
import jax.numpy as jnp
from jax import lax
from jax.experimental import pallas as pl
from jax.experimental.pallas import tpu as pltpu
from jax.sharding import PartitionSpec as P

MESH = pl.DeviceIdType.MESH
F32 = jnp.float32
BF16 = jnp.bfloat16
LOW = -1e30


def nt_dot(a, b):
    return lax.dot_general(a, b, (((1,), (1,)), ((), ())), preferred_element_type=F32)


def kernel(
    pages, zs, sides, dims,
    gid, slen, tab, q_in, pk, pv, sk, sv, w_in, out,
    qv, q_all, kraw, vraw, stage, kd, vd, kr, vr, skv, svv, wl, wr, s_ref,
    acc_s, m_s, l_s, sendb, recvb, own_part, sfx, sfx_in, smc, slc, coef, fin, attn_all, a_f32, pf, part, pin,
    loc, q_ss, q_rs, kv_ss, kv_rs, w_ss, w_rs, x_ss, x_rs, o_ss, o_rs, a_ss, a_rs, p_ss, p_rs,
):
    rows, per_kv, hd, tokens, groups, sufp = dims
    chips = pages // 2
    lanes = 2 * rows * per_kv
    c2 = hd ** (-0.5) * math.log2(math.e)
    me = lax.axis_index("page")
    z = lax.axis_index("kvh")
    chip = me // 2
    core = me % 2
    other = 1 - core
    sib = chip * 2 + other

    n1 = chips // 2
    sx, sy = sides
    cx, cy = chip // sy, chip % sy

    far_first = sorted(range(1, chips), key=lambda k: -min(k // sy, sx - k // sy) - min(k % sy, sy - k % sy))

    def chip_to(k):
        return (cx + k // sy) % sx * sy + (cy + k % sy) % sy

    def chip_from(k):
        return (cx + sx - k // sy) % sx * sy + (cy + sy - k % sy) % sy

    def to_page(src, dst, ss, rs, page):
        return pltpu.make_async_remote_copy(
            src_ref=src, dst_ref=dst, send_sem=ss, recv_sem=rs,
            device_id={"page": page}, device_id_type=MESH)

    loads = [
        pltpu.make_async_copy(q_in, qv, loc.at[0]),
        pltpu.make_async_copy(sk, skv, loc.at[1]),
        pltpu.make_async_copy(sv, svv, loc.at[2]),
        pltpu.make_async_copy(w_in.at[pl.ds(core * wl.shape[0], wl.shape[0])], wl, loc.at[3]),
        pltpu.make_async_copy(q_in.at[:, pl.ds(core * per_kv, per_kv)], q_all.at[0, 0], loc.at[4]),
    ]
    kvl = []
    for g in range(groups):
        kvl.append(pltpu.make_async_copy(pk.at[g], kraw.at[g], loc.at[6 + 2 * g]))
        kvl.append(pltpu.make_async_copy(pv.at[g], vraw.at[g], loc.at[7 + 2 * g]))
    for copy in [loads[0], loads[4]] + kvl + loads[1:4]:
        copy.start()

    bar = pltpu.get_barrier_semaphore()

    @pl.loop(1, pages)
    def _(j):
        pl.semaphore_signal(bar, inc=1, device_id={"page": (me + j) % pages}, device_id_type=MESH)

    @pl.loop(1, zs)
    def _(j):
        for cc in range(2):
            pl.semaphore_signal(
                bar, inc=1, device_id={"kvh": (z + j) % zs, "page": chip * 2 + cc}, device_id_type=MESH)

    def kv_copy(g, i):
        return to_page((kd, vd)[i].at[g, other], (kr, vr)[i].at[g], kv_ss.at[2 * g + i], kv_rs.at[2 * g + i], sib)

    for g in range(groups):
        for i in range(2):
            kvl[2 * g + i].wait()
            stage[...] = (kraw, vraw)[i][g].astype(F32)
            for kv in range(2):
                (kd, vd)[i][g, kv] = stage[pl.ds(kv, tokens, stride=2), :].astype(BF16)

    pl.semaphore_wait(bar, pages - 1 + 2 * (zs - 1))

    def q_copy(k, rc):
        kv = other if rc else core
        return to_page(
            q_in.at[:, pl.ds(kv * per_kv, per_kv)], q_all.at[k, rc],
            q_ss.at[2 * k + rc], q_rs.at[2 * k + rc], chip_to(k) * 2 + kv)

    for k in far_first:
        q_copy(k, 0).start()
        q_copy(k, 1).start()
    q_copy(0, 1).start()

    def count(r, c):
        g = gid[r]
        return tuple(c[e] + (g <= e).astype(jnp.int32) for e in range(groups - 1))

    first = lax.fori_loop(0, rows * pages, count, (jnp.int32(0),) * (groups - 1))
    btile = [jnp.minimum(f // (2 * rows), chips - 1) for f in first]
    bslot = [(cx + sx - b // sy) % sx * sy + (cy + sy - b % sy) % sy for b in btile]

    for g in range(groups):
        for i in range(2):
            kv_copy(g, i).start()

    def w_copy():
        return to_page(w_in.at[pl.ds(other * wl.shape[0], wl.shape[0])], wr, w_ss, w_rs, sib)

    w_copy().start()

    span = sufp * skv.shape[1]
    both = 2 * per_kv
    col = lax.broadcasted_iota(jnp.int32, (both, span), 1)
    row = lax.broadcasted_iota(jnp.int32, (both, span), 0)
    mine = (col % 2) == (row // per_kv)
    token = col // 2
    for copy in loads[:3]:
        copy.wait()
    for r in range(rows):
        pgs = [tab[r, j] % skv.shape[0] for j in range(sufp)]
        keys = jnp.concatenate([skv[pg] for pg in pgs], axis=0)
        vals = jnp.concatenate([svv[pg] for pg in pgs], axis=0)
        live = mine & (token < slen[r])
        s = jnp.where(live, nt_dot(qv[r], keys) * c2, LOW)
        top = jnp.max(s, axis=1, keepdims=True)
        p = jnp.where(live, jnp.exp2(s - top), 0.0)
        tot = jnp.sum(p, axis=1, keepdims=True)
        o = jnp.dot(p.astype(BF16), vals, preferred_element_type=F32)
        for kv in range(2):
            a, b = kv * per_kv, (kv + 1) * per_kv
            sfx[kv, r * per_kv:(r + 1) * per_kv, :] = o[a:b]
            smc[kv, r * per_kv:(r + 1) * per_kv, :] = jnp.broadcast_to(top[a:b], (per_kv, 128))
            slc[kv, r * per_kv:(r + 1) * per_kv, :] = jnp.broadcast_to(tot[a:b], (per_kv, 128))
    half = rows * per_kv
    hrow = lax.broadcasted_iota(jnp.int32, (half, 128), 0)
    hlane = lax.broadcasted_iota(jnp.int32, (half, 128), 1)
    sub8 = lax.broadcasted_iota(jnp.int32, (8, 128), 0)
    lane8 = lax.broadcasted_iota(jnp.int32, (8, 128), 1)
    for kv in range(2):
        side = jnp.where(core == kv, 0, 1)
        held = (lane8 // half) == side
        diag = hlane == hrow + side * half
        mrow = jnp.sum(jnp.where(diag, smc[kv], 0.0), axis=0, keepdims=True)
        lrow = jnp.sum(jnp.where(diag, slc[kv], 0.0), axis=0, keepdims=True)
        block = jnp.where(sub8 == 0, mrow, jnp.where(sub8 == 1, lrow, 0.0))
        sfx[kv, half:half + 8, :] = jnp.where(held, block, jnp.where(sub8 == 0, LOW, 0.0))

    def x_copy():
        return to_page(sfx.at[other], sfx_in, x_ss, x_rs, sib)

    x_copy().start()

    def o_copy(dst_chip, src_chip):
        return to_page(sendb.at[dst_chip], recvb.at[src_chip], o_ss.at[dst_chip], o_rs.at[src_chip], dst_chip * 2 + core)

    prow = lax.broadcasted_iota(jnp.int32, (lanes, 128), 0)
    plane = lax.broadcasted_iota(jnp.int32, (lanes, 128), 1)
    nb = groups - 1

    def tile_of(k):
        return k, gid[chip_from(k) * (2 * rows)]

    def q_wait(k):
        for rc in range(2):
            q_copy(k, rc).wait_recv()

    def columns(f, x):
        return functools.reduce(f, [x[:, i * 128:(i + 1) * 128] for i in range(tokens // 128)] if tokens > 128 else [x])

    def advance(now, then, slot, top_in):
        if now is not None:
            top = (jnp.max(top_in, axis=1, keepdims=True) * c2).astype(BF16).astype(F32)
        if then is not None:
            q = q_all[then[0]].reshape(lanes, hd)
        o, tot, top_out = None, None, None
        for i in range(2):
            part_of = slice(i * tokens, (i + 1) * tokens)
            if then is not None:
                x = nt_dot(q, kr[then[1]] if i else kd[then[1], core])
                s_ref[1 - slot, :, part_of] = x
                m = columns(jnp.maximum, x)
                top_out = m if i == 0 else jnp.maximum(top_out, m)
            if now is not None:
                p = jnp.exp2(s_ref[slot, :, part_of] * c2 - top)
                l = columns(jnp.add, p)
                tot = l if i == 0 else tot + l
                d = jnp.dot(p.astype(BF16), vr[now] if i else vd[now, core], preferred_element_type=F32)
                o = d if i == 0 else o + d
        if now is None:
            return top_out
        return top_out, o, top, jnp.sum(tot, axis=1, keepdims=True)

    def keep(at, o, top, tot):
        acc_s[at] = o
        m_s[at] = jnp.broadcast_to(top, (lanes, 128))
        l_s[at] = jnp.broadcast_to(tot, (lanes, 128))

    def finish(k, slot, dst, at):
        first_row = chip_from(k) * (2 * rows)
        g_low = gid[first_row]
        mc, lc = [], []
        for r in range(2 * rows):
            g_r = gid[first_row + (core if r < rows else other) * rows + r % rows]
            src = jnp.where(g_r == g_low, slot, jnp.maximum(g_r - 1, 0))
            a, b = r * per_kv, (r + 1) * per_kv
            dst[at, a:b, :] = acc_s[src, a:b, :].astype(BF16)
            mc.append(m_s[src, a:b, :])
            lc.append(l_s[src, a:b, :])
        mrow = jnp.sum(jnp.where(prow == plane, jnp.concatenate(mc, axis=0), 0.0), axis=0, keepdims=True)
        lrow = jnp.sum(jnp.where(prow == plane, jnp.concatenate(lc, axis=0), 0.0), axis=0, keepdims=True)
        high = lrow.astype(BF16).astype(F32)
        sub = lax.broadcasted_iota(jnp.int32, (16, 128), 0)
        block = jnp.where(sub == 0, mrow, jnp.where(sub == 1, high, jnp.where(sub == 2, lrow - high, 0.0)))
        dst[at, lanes:lanes + 16, :] = block.astype(BF16)

    def send(k):
        o_copy(chip_from(k), chip).start()

    def run(first_k, count, side, top, body):
        def two(i, top):
            k = first_k + 2 * i
            return body(k + 1, 1 - side, body(k, side, top))

        pairs = (count - 1) // 2
        top = lax.fori_loop(0, pairs, two, top)
        for k in range(2 * pairs, count):
            top = body(first_k + k, side, top, k == count - 1)
            side = 1 - side
        return side, top

    loads[4].wait()
    q_copy(0, 1).wait_recv()
    for g in range(groups):
        for i in range(2):
            kv_copy(g, i).wait_recv()
    top = advance(None, tile_of(0), 1, None)

    def before(k, slot, top, last=False):
        if last:
            for j in range(n1, chips):
                q_wait(j)
            then = (bslot[0], 1)
        else:
            q_wait(k + 1)
            then = tile_of(k + 1)
        top, *res = advance(tile_of(k)[1], then, slot, top)
        keep(nb + k, *res)
        return top

    slot = 0
    for k in range(n1):
        top = before(k, slot, top, k == n1 - 1)
        slot = 1 - slot

    for e in range(nb):
        then = (bslot[e + 1], e + 2) if e + 1 < nb else tile_of(n1)
        top, *res = advance(e + 1, then, slot, top)
        keep(e, *res)
        slot = 1 - slot

    @pl.loop(0, n1 - 1)
    def _(j):
        k = n1 - 1 - j
        finish(k, nb + k, sendb, chip_from(k))
        send(k)

    finish(0, nb, own_part, 0)

    def after(k, slot, top, last=False):
        top, *res = advance(tile_of(k)[1], None if last else tile_of(k + 1), slot, top)
        keep(nb, *res)
        finish(k, nb, sendb, chip_from(k))
        send(k)
        return top

    run(n1, chips - n1, slot, top, after)

    x_copy().wait_recv()

    @pl.loop(1, chips)
    def _(j):
        o_copy(chip, (chip + j) % chips).wait_recv()

    def partial(i, part_rows):
        return (recvb[(chip + i) % chips, part_rows, :] if i else own_part[0, part_rows, :]).astype(F32)

    ms, ls = [], []
    for i in range(chips):
        block = partial(i, slice(lanes, lanes + 16))
        ms.append(block[0:1])
        ls.append(block[1:2] + block[2:3])
    for block in (sfx[core, half:half + 8, :], sfx_in[half:half + 8, :]):
        ms.append(block[0:1])
        ls.append(block[1:2])
    peak = functools.reduce(jnp.maximum, ms)
    ws = [jnp.exp2(m - peak) for m in ms]
    inv = 1.0 / sum(a * b for a, b in zip(ws, ls))
    coef[...] = jnp.zeros_like(coef)
    for i, a in enumerate(ws):
        coef[i:i + 1, :] = a * inv
    ct = coef[...].T
    acc = jnp.zeros((lanes, hd), F32)
    for i in range(chips):
        acc += ct[:, i:i + 1] * partial(i, slice(0, lanes))
    mo = pl.ds(pl.multiple_of(core * half, half), half)
    so = pl.ds(pl.multiple_of(other * half, half), half)
    fin[mo, :] = acc[:half] + ct[:half, chips:chips + 1] * sfx[core, :half, :]
    fin[so, :] = acc[half:] + ct[half:, chips + 1:chips + 2] * sfx_in[:half, :]
    for h in range(per_kv):
        attn_all[0, :, h * hd:(h + 1) * hd] = fin[pl.ds(h, 2 * rows, stride=per_kv), :].astype(BF16)

    def a_copy(k):
        return to_page(attn_all.at[0], attn_all.at[k], a_ss.at[k], a_rs.at[k], chip_to(k) * 2 + core)

    for k in far_first:
        a_copy(k).start()

    loads[3].wait()
    w_copy().wait_recv()
    zrows = out.shape[0]
    pin[z * 2 + core] = jnp.zeros(pin.shape[1:], BF16)

    def p_copy(dst_z, dst_core, src_z, src_core):
        return pltpu.make_async_remote_copy(
            src_ref=part.at[dst_z * 2 + dst_core], dst_ref=pin.at[src_z * 2 + src_core],
            send_sem=p_ss.at[dst_z * 2 + dst_core], recv_sem=p_rs.at[src_z * 2 + src_core],
            device_id={"kvh": dst_z, "page": chip * 2 + dst_core}, device_id_type=MESH)

    def one_block(dx):
        zb = (cx + sx - dx) % sx
        for dy in range(sy):
            at = (cy + sy - dy) % sy * (2 * rows)
            a_f32[pl.ds(pl.multiple_of(at, 2 * rows), 2 * rows), :] = attn_all[dx * sy + dy].astype(F32)
        a = a_f32[...].astype(BF16)
        part[zb * 2 + other] = jnp.dot(a, wr[...], preferred_element_type=F32).astype(BF16)
        p_copy(zb, other, z, core).start()
        y = jnp.dot(a, wl[...], preferred_element_type=F32)
        part[zb * 2 + core] = y.astype(BF16)

        @pl.when(zb != z)
        def _():
            p_copy(zb, core, z, core).start()

        @pl.when(zb == z)
        def _():
            pf[...] = y

    for dy in range(1, sy):
        a_copy(dy).wait_recv()
    one_block(0)

    for dx in sorted(range(1, sx), key=lambda d: min(d, sx - d)):
        for dy in range(sy):
            a_copy(dx * sy + dy).wait_recv()
        one_block(dx)

    @pl.loop(0, zs)
    def _(j):
        p_copy(z, core, (z + j) % zs, other).wait_recv()

    @pl.loop(1, zs)
    def _(j):
        p_copy(z, core, (z + j) % zs, core).wait_recv()

    total = pf[...]
    for i in range(2 * zs):
        total += pin[i].astype(F32)
    out[...] = total.astype(BF16)

    q_copy(0, 1).wait_send()

    for k in range(1, chips):
        q_copy(k, 0).wait_send()
        q_copy(k, 1).wait_send()
        a_copy(k).wait_send()

    for g in range(groups):
        for i in range(2):
            kv_copy(g, i).wait_send()
    w_copy().wait_send()
    x_copy().wait_send()

    @pl.loop(1, chips)
    def _(j):
        o_copy((chip + j) % chips, chip).wait_send()

    @pl.loop(0, zs)
    def _(j):
        p_copy((z + j) % zs, other, z, core).wait_send()

    @pl.loop(1, zs)
    def _(j):
        p_copy((z + j) % zs, core, z, core).wait_send()


def on_device(pages, zs, queries, gid, slen, tab, pk, pv, sk, sv, w):
    rows, heads, hd = queries.shape
    groups, tokens, kvs = pk.shape[:3]
    per_kv = heads // kvs
    pool, plen = sk.shape[:2]
    sufp = tab.shape[1]
    chips = pages // 2
    side = math.isqrt(chips)
    side = side if side * side == chips else 1
    lanes = 2 * rows * per_kv
    half = rows * per_kv
    kept = groups - 1 + chips // 2
    feats, cols = w.shape
    fh = feats // 2
    zrows = rows * pages // zs
    pk = pk.reshape(groups, tokens * kvs, hd)
    pv = pv.reshape(groups, tokens * kvs, hd)
    sk = sk.reshape(pool, plen * kvs, hd)
    sv = sv.reshape(pool, plen * kvs, hd)
    V, D = pltpu.VMEM, pltpu.SemaphoreType.DMA
    smem = pl.BlockSpec(memory_space=pltpu.SMEM)
    anym = pl.BlockSpec(memory_space=pl.ANY)
    scratch = [
        V((rows, heads, hd), BF16), V((chips, 2, rows, per_kv, hd), BF16),
        V((groups, 2 * tokens, hd), BF16), V((groups, 2 * tokens, hd), BF16), V((2 * tokens, hd), F32),
        V((groups, 2, tokens, hd), BF16), V((groups, 2, tokens, hd), BF16),
        V((groups, tokens, hd), BF16), V((groups, tokens, hd), BF16),
        V((pool, plen * kvs, hd), BF16), V((pool, plen * kvs, hd), BF16),
        V((fh, cols), BF16), V((fh, cols), BF16), V((2, lanes, 2 * tokens), F32),
        V((kept, lanes, hd), F32), V((kept, lanes, 128), F32), V((kept, lanes, 128), F32),
        V((chips, lanes + 16, hd), BF16), V((chips, lanes + 16, hd), BF16), V((1, lanes + 16, hd), BF16),
        V((2, half + 8, hd), F32), V((half + 8, hd), F32), V((2, half, 128), F32), V((2, half, 128), F32),
        V((128, 128), F32), V((lanes, hd), F32), V((chips, 2 * rows, fh), BF16), V((zrows, fh), F32),
        V((zrows, cols), F32), V((2 * zs, zrows, cols), BF16), V((2 * zs, zrows, cols), BF16),
        D((6 + 2 * groups,)), D((pages,)), D((pages,)), D((2 * groups,)), D((2 * groups,)), D, D, D, D,
        D((chips,)), D((chips,)), D((chips,)), D((chips,)), D((2 * zs,)), D((2 * zs,)),
    ]
    dims = (rows, per_kv, hd, tokens, groups, sufp)
    return pl.pallas_call(
        functools.partial(kernel, pages, zs, (side, chips // side), dims),
        out_shape=jax.ShapeDtypeStruct((zrows, cols), BF16),
        in_specs=[smem] * 3 + [anym] * 6,
        out_specs=pl.BlockSpec(memory_space=pltpu.VMEM),
        scratch_shapes=scratch,
        compiler_params=pltpu.CompilerParams(
            collective_id=0, has_side_effects=True, vmem_limit_bytes=56 * 1024 * 1024),
    )(gid, slen, tab, queries, pk, pv, sk, sv, w)


def solution(mesh):
    placed = (
        P("page", "kvh", None), P(), P("page"), P("page", None),
        P(None, "page", "kvh", None), P(None, "page", "kvh", None),
        P("page", None, "kvh", None), P("page", None, "kvh", None), P("kvh", "page"),
    )
    return jax.shard_map(
        functools.partial(on_device, mesh.shape["page"], mesh.shape["kvh"]),
        mesh=mesh, in_specs=placed, out_specs=P("kvh", "page"), check_vma=False)
```

```python
import functools
import math

import jax
import jax.numpy as jnp
from jax import lax
from jax.experimental import pallas as pl
from jax.experimental.pallas import tpu as pltpu
from jax.sharding import PartitionSpec as P

MESH = pl.DeviceIdType.MESH
F32 = jnp.float32
BF16 = jnp.bfloat16
LOW = -1e30


def nt_dot(a, b):
    return lax.dot_general(a, b, (((1,), (1,)), ((), ())), preferred_element_type=F32)


def kernel(
    pages, zs, sides, dims,
    gid, slen, tab, q_in, pk, pv, sk, sv, w_in, out,
    qv, q_all, kraw, vraw, stage, kd, vd, kr, vr, skv, svv, wl, wr, s_ref,
    acc_s, m_s, l_s, sendb, recvb, own_part, sfx, sfx_in, smc, slc, coef, fin, attn_all, a_mat, pf, part, pin,
    loc, q_ss, q_rs, kv_ss, kv_rs, w_ss, w_rs, x_ss, x_rs, o_ss, o_rs, a_ss, a_rs, p_ss, p_rs,
):
    rows, per_kv, hd, tokens, groups, sufp = dims
    chips = pages // 2
    lanes = 2 * rows * per_kv
    c2 = hd ** (-0.5) * math.log2(math.e)
    me = lax.axis_index("page")
    z = lax.axis_index("kvh")
    chip = me // 2
    core = me % 2
    other = 1 - core
    sib = chip * 2 + other
    sx, sy = sides
    cx, cy = chip // sy, chip % sy
    far_first = sorted(range(1, chips), key=lambda k: -min(k // sy, sx - k // sy) - min(k % sy, sy - k % sy))

    def chip_at(dx, dy):
        return (cx + dx) % sx * sy + (cy + dy) % sy

    def peer(j):
        dx, dy = (jnp.where(i < n // 2, n // 2 + i, n - 1 - i) for i, n in ((j // sy, sx), (j % sy, sy)))
        return chip_at(dx, dy)

    def to_page(src, dst, ss, rs, page):
        return pltpu.make_async_remote_copy(
            src_ref=src, dst_ref=dst, send_sem=ss, recv_sem=rs,
            device_id={"page": page}, device_id_type=MESH)

    bar = pltpu.get_barrier_semaphore()

    @pl.loop(1, pages)
    def _(j):
        pl.semaphore_signal(bar, inc=1, device_id={"page": (me + j) % pages}, device_id_type=MESH)

    @pl.loop(1, zs)
    def _(j):
        for cc in range(2):
            pl.semaphore_signal(
                bar, inc=1, device_id={"kvh": (z + j) % zs, "page": chip * 2 + cc}, device_id_type=MESH)

    loads = [
        pltpu.make_async_copy(q_in, qv, loc.at[0]),
        pltpu.make_async_copy(sk, skv, loc.at[1]),
        pltpu.make_async_copy(sv, svv, loc.at[2]),
        pltpu.make_async_copy(w_in.at[pl.ds(core * wl.shape[0], wl.shape[0])], wl, loc.at[3]),
        pltpu.make_async_copy(q_in.at[:, pl.ds(core * per_kv, per_kv)], q_all.at[chip, core], loc.at[4]),
    ]
    kvl = []
    for g in range(groups):
        kvl.append(pltpu.make_async_copy(pk.at[g], kraw.at[g], loc.at[6 + 2 * g]))
        kvl.append(pltpu.make_async_copy(pv.at[g], vraw.at[g], loc.at[7 + 2 * g]))
    for copy in [loads[0], loads[4]] + kvl + loads[1:4]:
        copy.start()

    pl.semaphore_wait(bar, pages - 1 + 2 * (zs - 1))

    def q_copy(page, src_page):
        kv = page % 2
        return to_page(
            q_in.at[:, pl.ds(kv * per_kv, per_kv)], q_all.at[src_page // 2, src_page % 2],
            q_ss.at[page], q_rs.at[src_page], page)

    for k in far_first:
        for cc in range(2):
            q_copy(chip_at(k // sy, k % sy) * 2 + cc, me).start()
    q_copy(sib, me).start()

    def count(r, c):
        g = gid[r]
        return tuple(c[e] + (g <= e).astype(jnp.int32) for e in range(groups - 1))

    first = lax.fori_loop(0, rows * pages, count, (jnp.int32(0),) * (groups - 1))
    btile = [jnp.minimum(f // (2 * rows), chips - 1) for f in first]

    def kv_copy(g, i):
        return to_page((kd, vd)[i].at[g, other], (kr, vr)[i].at[g], kv_ss.at[2 * g + i], kv_rs.at[2 * g + i], sib)

    for g in range(groups):
        for i in range(2):
            kvl[2 * g + i].wait()
            stage[...] = (kraw, vraw)[i][g].astype(F32)
            for kv in range(2):
                (kd, vd)[i][g, kv] = stage[pl.ds(kv, tokens, stride=2), :].astype(BF16)
            kv_copy(g, i).start()

    def w_copy():
        return to_page(w_in.at[pl.ds(other * wl.shape[0], wl.shape[0])], wr, w_ss, w_rs, sib)

    w_copy().start()

    span = sufp * skv.shape[1]
    both = 2 * per_kv
    col = lax.broadcasted_iota(jnp.int32, (both, span), 1)
    row = lax.broadcasted_iota(jnp.int32, (both, span), 0)
    mine = (col % 2) == (row // per_kv)
    token = col // 2
    for copy in loads[:3]:
        copy.wait()
    for r in range(rows):
        pgs = [tab[r, j] % skv.shape[0] for j in range(sufp)]
        keys = jnp.concatenate([skv[pg] for pg in pgs], axis=0)
        vals = jnp.concatenate([svv[pg] for pg in pgs], axis=0)
        live = mine & (token < slen[r])
        s = jnp.where(live, nt_dot(qv[r], keys) * c2, LOW)
        top = jnp.max(s, axis=1, keepdims=True)
        p = jnp.where(live, jnp.exp2(s - top), 0.0)
        tot = jnp.sum(p, axis=1, keepdims=True)
        o = jnp.dot(p.astype(BF16), vals, preferred_element_type=F32)
        for kv in range(2):
            a, b = kv * per_kv, (kv + 1) * per_kv
            sfx[kv, r * per_kv:(r + 1) * per_kv, :] = o[a:b]
            smc[kv, r * per_kv:(r + 1) * per_kv, :] = jnp.broadcast_to(top[a:b], (per_kv, 128))
            slc[kv, r * per_kv:(r + 1) * per_kv, :] = jnp.broadcast_to(tot[a:b], (per_kv, 128))
    half = rows * per_kv
    hrow = lax.broadcasted_iota(jnp.int32, (half, 128), 0) + core * half
    hlane = lax.broadcasted_iota(jnp.int32, (half, 128), 1)
    sub8 = lax.broadcasted_iota(jnp.int32, (8, 128), 0)
    lane8 = lax.broadcasted_iota(jnp.int32, (8, 128), 1)
    held = (lane8 // half) == core
    for kv in range(2):
        mrow = jnp.sum(jnp.where(hrow == hlane, smc[kv], 0.0), axis=0, keepdims=True)
        lrow = jnp.sum(jnp.where(hrow == hlane, slc[kv], 0.0), axis=0, keepdims=True)
        block = jnp.where(sub8 == 0, mrow, jnp.where(sub8 == 1, lrow, 0.0))
        sfx[kv, half:half + 8, :] = jnp.where(held, block, jnp.where(sub8 == 0, LOW, 0.0))

    def x_copy():
        return to_page(sfx.at[other], sfx_in, x_ss, x_rs, sib)

    x_copy().start()

    loads[4].wait()

    @pl.loop(1, pages)
    def _(j):
        q_copy(me, (me + j) % pages).wait_recv()

    for g in range(groups):
        for i in range(2):
            kv_copy(g, i).wait_recv()

    def o_copy(dst_chip, src_chip):
        return to_page(sendb.at[dst_chip], recvb.at[src_chip], o_ss.at[dst_chip], o_rs.at[src_chip], dst_chip * 2 + core)

    prow = lax.broadcasted_iota(jnp.int32, (lanes, 128), 0)
    plane = lax.broadcasted_iota(jnp.int32, (lanes, 128), 1)
    nb = groups - 1

    def tile_of(k):
        t = peer(k)
        return t, gid[t * (2 * rows)]

    def columns(f, x):
        return functools.reduce(f, [x[:, i * 128:(i + 1) * 128] for i in range(tokens // 128)] if tokens > 128 else [x])

    def advance(now, then, slot, top_in):
        if now is not None:
            top = (jnp.max(top_in, axis=1, keepdims=True) * c2).astype(BF16).astype(F32)
        if then is not None:
            q = q_all[then[0]].reshape(lanes, hd)
        o, tot, top_out = None, None, None
        for i in range(2):
            part_of = slice(i * tokens, (i + 1) * tokens)
            if then is not None:
                x = nt_dot(q, kr[then[1]] if i else kd[then[1], core])
                s_ref[1 - slot, :, part_of] = x
                m = columns(jnp.maximum, x)
                top_out = m if i == 0 else jnp.maximum(top_out, m)
            if now is not None:
                p = jnp.exp2(s_ref[slot, :, part_of] * c2 - top)
                l = columns(jnp.add, p)
                tot = l if i == 0 else tot + l
                d = jnp.dot(p.astype(BF16), vr[now] if i else vd[now, core], preferred_element_type=F32)
                o = d if i == 0 else o + d
        if now is None:
            return top_out
        return top_out, o, top, jnp.sum(tot, axis=1, keepdims=True)

    def keep(at, o, top, tot):
        acc_s[at] = o
        m_s[at] = jnp.broadcast_to(top, (lanes, 128))
        l_s[at] = jnp.broadcast_to(tot, (lanes, 128))

    def finish(k, dst, at):
        t, g_low = tile_of(k)
        mc, lc = [], []
        for r in range(2 * rows):
            g_r = gid[t * (2 * rows) + r]
            src = jnp.where(g_r == g_low, nb, jnp.maximum(g_r - 1, 0))
            a, b = r * per_kv, (r + 1) * per_kv
            dst[at, a:b, :] = acc_s[src, a:b, :].astype(BF16)
            mc.append(m_s[src, a:b, :])
            lc.append(l_s[src, a:b, :])
        mrow = jnp.sum(jnp.where(prow == plane, jnp.concatenate(mc, axis=0), 0.0), axis=0, keepdims=True)
        lrow = jnp.sum(jnp.where(prow == plane, jnp.concatenate(lc, axis=0), 0.0), axis=0, keepdims=True)
        high = lrow.astype(BF16).astype(F32)
        sub = lax.broadcasted_iota(jnp.int32, (16, 128), 0)
        block = jnp.where(sub == 0, mrow, jnp.where(sub == 1, high, jnp.where(sub == 2, lrow - high, 0.0)))
        dst[at, lanes:lanes + 16, :] = block.astype(BF16)

    top = advance(None, (btile[0], 1), 1, None)
    for e in range(nb):
        then = (btile[e + 1], e + 2) if e + 1 < nb else tile_of(0)
        top, *res = advance(e + 1, then, e % 2, top)
        keep(e, *res)
    base = nb % 2

    def one(k, slot, top, last=False):
        t, g = tile_of(k)
        top, *res = advance(g, None if last else tile_of(k + 1), slot, top)
        keep(nb, *res)
        if last:
            finish(k, own_part, 0)
        else:
            finish(k, sendb, t)
            o_copy(t, chip).start()
        return top

    def pair(i, top):
        return one(2 * i + 1, 1 - base, one(2 * i, base, top))

    top = lax.fori_loop(0, chips // 2 - 1, pair, top)
    top = one(chips - 2, base, top)
    one(chips - 1, 1 - base, top, last=True)

    x_copy().wait_recv()

    @pl.loop(1, chips)
    def _(j):
        o_copy(chip, (chip + j) % chips).wait_recv()

    def partial(i, part_rows):
        return (recvb[(chip + i) % chips, part_rows, :] if i else own_part[0, part_rows, :]).astype(F32)

    ms, ls = [], []
    for i in range(chips):
        block = partial(i, slice(lanes, lanes + 16))
        ms.append(block[0:1])
        ls.append(block[1:2] + block[2:3])
    for block in (sfx[core, half:half + 8, :], sfx_in[half:half + 8, :]):
        ms.append(block[0:1])
        ls.append(block[1:2])
    peak = functools.reduce(jnp.maximum, ms)
    ws = [jnp.exp2(m - peak) for m in ms]
    inv = 1.0 / sum(a * b for a, b in zip(ws, ls))
    coef[...] = jnp.zeros_like(coef)
    for i, a in enumerate(ws):
        coef[i:i + 1, :] = a * inv
    ct = coef[...].T
    acc = jnp.zeros((lanes, hd), F32)
    for i in range(chips):
        acc += ct[:, i:i + 1] * partial(i, slice(0, lanes))
    fin[...] = acc
    mo = pl.ds(pl.multiple_of(core * half, half), half)
    so = pl.ds(pl.multiple_of(other * half, half), half)
    smc[0] = jnp.where(core == 0, ct[:half, chips:chips + 1], ct[half:, chips:chips + 1]) * sfx[core, :half, :]
    smc[1] = jnp.where(core == 0, ct[half:, chips + 1:chips + 2], ct[:half, chips + 1:chips + 2]) * sfx_in[:half, :]
    fin[mo, :] += smc[0]
    fin[so, :] += smc[1]
    for h in range(per_kv):
        attn_all[chip, :, h * hd:(h + 1) * hd] = fin[pl.ds(h, 2 * rows, stride=per_kv), :].astype(BF16)

    def a_copy(dst_chip, src_chip):
        return to_page(
            attn_all.at[src_chip], attn_all.at[src_chip], a_ss.at[dst_chip], a_rs.at[src_chip], dst_chip * 2 + core)

    for k in far_first:
        a_copy(chip_at(k // sy, k % sy), chip).start()

    @pl.loop(1, pages)
    def _(j):
        q_copy((me + j) % pages, me).wait_send()

    for g in range(groups):
        for i in range(2):
            kv_copy(g, i).wait_send()
    w_copy().wait_send()
    x_copy().wait_send()

    @pl.loop(1, chips)
    def _(j):
        o_copy((chip + j) % chips, chip).wait_send()

    loads[3].wait()
    w_copy().wait_recv()
    zrows = out.shape[0]
    pin[z * 2 + core] = jnp.zeros(pin.shape[1:], BF16)

    @pl.loop(1, chips)
    def _(j):
        a_copy(chip, (chip + j) % chips).wait_recv()

    for i in range(chips // 2):
        pair = jnp.concatenate([attn_all[2 * i].astype(F32), attn_all[2 * i + 1].astype(F32)], axis=0)
        a_mat[i * 4 * rows:(i + 1) * 4 * rows, :] = pair.astype(BF16)

    def p_copy(dst_z, dst_core, src_z, src_core):
        return pltpu.make_async_remote_copy(
            src_ref=part.at[dst_z * 2 + dst_core], dst_ref=pin.at[src_z * 2 + src_core],
            send_sem=p_ss.at[dst_z * 2 + dst_core], recv_sem=p_rs.at[src_z * 2 + src_core],
            device_id={"kvh": dst_z, "page": chip * 2 + dst_core}, device_id_type=MESH)

    y = jnp.dot(a_mat[...], wr[...], preferred_element_type=F32)
    for k in range(zs):
        part[k * 2 + other] = y[k * zrows:(k + 1) * zrows].astype(BF16)

    @pl.loop(0, zs)
    def _(j):
        p_copy((z + j) % zs, other, z, core).start()

    y = jnp.dot(a_mat[...], wl[...], preferred_element_type=F32)
    pf[...] = y
    for k in range(zs):
        part[k * 2 + core] = y[k * zrows:(k + 1) * zrows].astype(BF16)

    @pl.loop(1, zs)
    def _(j):
        p_copy((z + j) % zs, core, z, core).start()

    @pl.loop(1, chips)
    def _(j):
        a_copy((chip + j) % chips, chip).wait_send()

    @pl.loop(0, zs)
    def _(j):
        p_copy(z, core, (z + j) % zs, other).wait_recv()

    @pl.loop(1, zs)
    def _(j):
        p_copy(z, core, (z + j) % zs, core).wait_recv()

    total = pf[pl.ds(pl.multiple_of(z * zrows, zrows), zrows), :]
    for i in range(2 * zs):
        total += pin[i].astype(F32)
    out[...] = total.astype(BF16)

    @pl.loop(0, zs)
    def _(j):
        p_copy((z + j) % zs, other, z, core).wait_send()

    @pl.loop(1, zs)
    def _(j):
        p_copy((z + j) % zs, core, z, core).wait_send()


def on_device(pages, zs, queries, gid, slen, tab, pk, pv, sk, sv, w):
    rows, heads, hd = queries.shape
    groups, tokens, kvs = pk.shape[:3]
    per_kv = heads // kvs
    pool, plen = sk.shape[:2]
    sufp = tab.shape[1]
    chips = pages // 2
    side = math.isqrt(chips)
    side = side if side * side == chips else 1
    lanes = 2 * rows * per_kv
    half = rows * per_kv
    feats, cols = w.shape
    fh = feats // 2
    zrows = rows * pages // zs
    pk = pk.reshape(groups, tokens * kvs, hd)
    pv = pv.reshape(groups, tokens * kvs, hd)
    sk = sk.reshape(pool, plen * kvs, hd)
    sv = sv.reshape(pool, plen * kvs, hd)
    V, D = pltpu.VMEM, pltpu.SemaphoreType.DMA
    smem = pl.BlockSpec(memory_space=pltpu.SMEM)
    anym = pl.BlockSpec(memory_space=pl.ANY)
    scratch = [
        V((rows, heads, hd), BF16), V((chips, 2, rows, per_kv, hd), BF16),
        V((groups, 2 * tokens, hd), BF16), V((groups, 2 * tokens, hd), BF16), V((2 * tokens, hd), F32),
        V((groups, 2, tokens, hd), BF16), V((groups, 2, tokens, hd), BF16),
        V((groups, tokens, hd), BF16), V((groups, tokens, hd), BF16),
        V((pool, plen * kvs, hd), BF16), V((pool, plen * kvs, hd), BF16),
        V((fh, cols), BF16), V((fh, cols), BF16), V((2, lanes, 2 * tokens), F32),
        V((groups, lanes, hd), F32), V((groups, lanes, 128), F32), V((groups, lanes, 128), F32),
        V((chips, lanes + 16, hd), BF16), V((chips, lanes + 16, hd), BF16), V((1, lanes + 16, hd), BF16),
        V((2, half + 8, hd), F32), V((half + 8, hd), F32), V((2, half, 128), F32), V((2, half, 128), F32),
        V((128, 128), F32), V((lanes, hd), F32), V((chips, 2 * rows, fh), BF16), V((rows * pages, fh), BF16),
        V((rows * pages, cols), F32), V((2 * zs, zrows, cols), BF16), V((2 * zs, zrows, cols), BF16),
        D((6 + 2 * groups,)), D((pages,)), D((pages,)), D((2 * groups,)), D((2 * groups,)), D, D, D, D,
        D((chips,)), D((chips,)), D((chips,)), D((chips,)), D((2 * zs,)), D((2 * zs,)),
    ]
    dims = (rows, per_kv, hd, tokens, groups, sufp)
    return pl.pallas_call(
        functools.partial(kernel, pages, zs, (side, chips // side), dims),
        out_shape=jax.ShapeDtypeStruct((zrows, cols), BF16),
        in_specs=[smem] * 3 + [anym] * 6,
        out_specs=pl.BlockSpec(memory_space=pltpu.VMEM),
        scratch_shapes=scratch,
        compiler_params=pltpu.CompilerParams(
            collective_id=0, has_side_effects=True, vmem_limit_bytes=56 * 1024 * 1024),
    )(gid, slen, tab, queries, pk, pv, sk, sv, w)


def solution(mesh):
    placed = (
        P("page", "kvh", None), P(), P("page"), P("page", None),
        P(None, "page", "kvh", None), P(None, "page", "kvh", None),
        P("page", None, "kvh", None), P("page", None, "kvh", None), P("kvh", "page"),
    )
    return jax.shard_map(
        functools.partial(on_device, mesh.shape["page"], mesh.shape["kvh"]),
        mesh=mesh, in_specs=placed, out_specs=P("kvh", "page"), check_vma=False)
```

```python
import functools
import math

import jax
import jax.numpy as jnp
from jax import lax
from jax.experimental import pallas as pl
from jax.experimental.pallas import tpu as pltpu
from jax.sharding import PartitionSpec as P

MESH = pl.DeviceIdType.MESH
F32 = jnp.float32
BF16 = jnp.bfloat16
LOW = -1e30


def nt_dot(a, b):
    return lax.dot_general(a, b, (((1,), (1,)), ((), ())), preferred_element_type=F32)


def kernel(
    pages, zs, sides, dims,
    gid, slen, tab, q_in, pk, pv, sk, sv, w_in, out,
    qv, q_all, kraw, vraw, stage, kd, vd, kr, vr, skv, svv, wl, wr, s_ref,
    acc_s, m_s, l_s, sendb, recvb, own_part, sfx, sfx_in, smc, slc, coef, fin, attn_all, a_f32, pf, part, pin,
    loc, q_ss, q_rs, kv_ss, kv_rs, w_ss, w_rs, x_ss, x_rs, o_ss, o_rs, a_ss, a_rs, p_ss, p_rs,
):
    rows, per_kv, hd, tokens, groups, sufp = dims
    chips = pages // 2
    lanes = 2 * rows * per_kv
    c2 = hd ** (-0.5) * math.log2(math.e)
    me = lax.axis_index("page")
    z = lax.axis_index("kvh")
    chip = me // 2
    core = me % 2
    other = 1 - core
    sib = chip * 2 + other

    sx, sy = sides
    n1 = sy
    cx, cy = chip // sy, chip % sy

    far_first = sorted(range(1, chips), key=lambda k: -min(k // sy, sx - k // sy) - min(k % sy, sy - k % sy))

    def chip_to(k):
        return (cx + k // sy) % sx * sy + (cy + k % sy) % sy

    def chip_from(k):
        return (cx + sx - k // sy) % sx * sy + (cy + sy - k % sy) % sy

    def to_page(src, dst, ss, rs, page):
        return pltpu.make_async_remote_copy(
            src_ref=src, dst_ref=dst, send_sem=ss, recv_sem=rs,
            device_id={"page": page}, device_id_type=MESH)

    bar = pltpu.get_barrier_semaphore()

    @pl.loop(1, pages)
    def _(j):
        pl.semaphore_signal(bar, inc=1, device_id={"page": (me + j) % pages}, device_id_type=MESH)

    @pl.loop(1, zs)
    def _(j):
        for cc in range(2):
            pl.semaphore_signal(
                bar, inc=1, device_id={"kvh": (z + j) % zs, "page": chip * 2 + cc}, device_id_type=MESH)

    loads = [
        pltpu.make_async_copy(q_in, qv, loc.at[0]),
        pltpu.make_async_copy(sk, skv, loc.at[1]),
        pltpu.make_async_copy(sv, svv, loc.at[2]),
        pltpu.make_async_copy(w_in.at[pl.ds(core * wl.shape[0], wl.shape[0])], wl, loc.at[3]),
        pltpu.make_async_copy(q_in.at[:, pl.ds(core * per_kv, per_kv)], q_all.at[0, 0], loc.at[4]),
    ]
    kvl = []
    for g in range(groups):
        kvl.append(pltpu.make_async_copy(pk.at[g], kraw.at[g], loc.at[6 + 2 * g]))
        kvl.append(pltpu.make_async_copy(pv.at[g], vraw.at[g], loc.at[7 + 2 * g]))
    for copy in [loads[0], loads[4]] + kvl + loads[1:4]:
        copy.start()

    def kv_copy(g, i):
        return to_page((kd, vd)[i].at[g, other], (kr, vr)[i].at[g], kv_ss.at[2 * g + i], kv_rs.at[2 * g + i], sib)

    for g in range(groups):
        for i in range(2):
            kvl[2 * g + i].wait()
            stage[...] = (kraw, vraw)[i][g].astype(F32)
            for kv in range(2):
                (kd, vd)[i][g, kv] = stage[pl.ds(kv, tokens, stride=2), :].astype(BF16)

    pl.semaphore_wait(bar, pages - 1 + 2 * (zs - 1))

    def q_copy(k, rc):
        kv = other if rc else core
        return to_page(
            q_in.at[:, pl.ds(kv * per_kv, per_kv)], q_all.at[k, rc],
            q_ss.at[2 * k + rc], q_rs.at[2 * k + rc], chip_to(k) * 2 + kv)

    for k in far_first:
        q_copy(k, 0).start()
        q_copy(k, 1).start()
    q_copy(0, 1).start()

    def count(r, c):
        g = gid[r]
        return tuple(c[e] + (g <= e).astype(jnp.int32) for e in range(groups - 1))

    first = lax.fori_loop(0, rows * pages, count, (jnp.int32(0),) * (groups - 1))
    btile = [jnp.minimum(f // (2 * rows), chips - 1) for f in first]
    bslot = [(cx + sx - b // sy) % sx * sy + (cy + sy - b % sy) % sy for b in btile]

    for g in range(groups):
        for i in range(2):
            kv_copy(g, i).start()

    def w_copy():
        return to_page(w_in.at[pl.ds(other * wl.shape[0], wl.shape[0])], wr, w_ss, w_rs, sib)

    w_copy().start()

    span = sufp * skv.shape[1]
    both = 2 * per_kv
    col = lax.broadcasted_iota(jnp.int32, (both, span), 1)
    row = lax.broadcasted_iota(jnp.int32, (both, span), 0)
    mine = (col % 2) == (row // per_kv)
    token = col // 2
    for copy in loads[:3]:
        copy.wait()
    for r in range(rows):
        pgs = [tab[r, j] % skv.shape[0] for j in range(sufp)]
        keys = jnp.concatenate([skv[pg] for pg in pgs], axis=0)
        vals = jnp.concatenate([svv[pg] for pg in pgs], axis=0)
        live = mine & (token < slen[r])
        s = jnp.where(live, nt_dot(qv[r], keys) * c2, LOW)
        top = jnp.max(s, axis=1, keepdims=True)
        p = jnp.where(live, jnp.exp2(s - top), 0.0)
        tot = jnp.sum(p, axis=1, keepdims=True)
        o = jnp.dot(p.astype(BF16), vals, preferred_element_type=F32)
        for kv in range(2):
            a, b = kv * per_kv, (kv + 1) * per_kv
            sfx[kv, r * per_kv:(r + 1) * per_kv, :] = o[a:b]
            smc[kv, r * per_kv:(r + 1) * per_kv, :] = jnp.broadcast_to(top[a:b], (per_kv, 128))
            slc[kv, r * per_kv:(r + 1) * per_kv, :] = jnp.broadcast_to(tot[a:b], (per_kv, 128))
    half = rows * per_kv
    hrow = lax.broadcasted_iota(jnp.int32, (half, 128), 0)
    hlane = lax.broadcasted_iota(jnp.int32, (half, 128), 1)
    sub8 = lax.broadcasted_iota(jnp.int32, (8, 128), 0)
    lane8 = lax.broadcasted_iota(jnp.int32, (8, 128), 1)
    for kv in range(2):
        side = jnp.where(core == kv, 0, 1)
        held = (lane8 // half) == side
        diag = hlane == hrow + side * half
        mrow = jnp.sum(jnp.where(diag, smc[kv], 0.0), axis=0, keepdims=True)
        lrow = jnp.sum(jnp.where(diag, slc[kv], 0.0), axis=0, keepdims=True)
        block = jnp.where(sub8 == 0, mrow, jnp.where(sub8 == 1, lrow, 0.0))
        sfx[kv, half:half + 8, :] = jnp.where(held, block, jnp.where(sub8 == 0, LOW, 0.0))

    def x_copy():
        return to_page(sfx.at[other], sfx_in, x_ss, x_rs, sib)

    x_copy().start()

    def o_copy(dst_chip, src_chip):
        return to_page(sendb.at[dst_chip], recvb.at[src_chip], o_ss.at[dst_chip], o_rs.at[src_chip], dst_chip * 2 + core)

    prow = lax.broadcasted_iota(jnp.int32, (lanes, 128), 0)
    plane = lax.broadcasted_iota(jnp.int32, (lanes, 128), 1)
    nb = groups - 1

    early = sorted(range(sy), key=lambda d: min(d, sy - d))

    def late(j):
        dx, dy = (jnp.where(i < n // 2, n // 2 + i, n - 1 - i) for i, n in ((j // sy, sx), (j % sy, sy)))
        return dx * sy + dy

    def tile_of(k):
        return k, gid[chip_from(k) * (2 * rows)]

    def q_wait(k):
        for rc in range(2):
            q_copy(k, rc).wait_recv()

    def columns(f, x):
        return functools.reduce(f, [x[:, i * 128:(i + 1) * 128] for i in range(tokens // 128)] if tokens > 128 else [x])

    def advance(now, then, slot, top_in):
        if now is not None:
            top = (jnp.max(top_in, axis=1, keepdims=True) * c2).astype(BF16).astype(F32)
        if then is not None:
            q = q_all[then[0]].reshape(lanes, hd)
        o, tot, top_out = None, None, None
        for i in range(2):
            part_of = slice(i * tokens, (i + 1) * tokens)
            if then is not None:
                x = nt_dot(q, kr[then[1]] if i else kd[then[1], core])
                s_ref[1 - slot, :, part_of] = x
                m = columns(jnp.maximum, x)
                top_out = m if i == 0 else jnp.maximum(top_out, m)
            if now is not None:
                p = jnp.exp2(s_ref[slot, :, part_of] * c2 - top)
                l = columns(jnp.add, p)
                tot = l if i == 0 else tot + l
                d = jnp.dot(p.astype(BF16), vr[now] if i else vd[now, core], preferred_element_type=F32)
                o = d if i == 0 else o + d
        if now is None:
            return top_out
        return top_out, o, top, jnp.sum(tot, axis=1, keepdims=True)

    def keep(at, o, top, tot):
        acc_s[at] = o
        m_s[at] = jnp.broadcast_to(top, (lanes, 128))
        l_s[at] = jnp.broadcast_to(tot, (lanes, 128))

    def finish(k, slot, dst, at):
        first_row = chip_from(k) * (2 * rows)
        g_low = gid[first_row]
        mc, lc = [], []
        for r in range(2 * rows):
            g_r = gid[first_row + (core if r < rows else other) * rows + r % rows]
            src = jnp.where(g_r == g_low, slot, jnp.maximum(g_r - 1, 0))
            a, b = r * per_kv, (r + 1) * per_kv
            dst[at, a:b, :] = acc_s[src, a:b, :].astype(BF16)
            mc.append(m_s[src, a:b, :])
            lc.append(l_s[src, a:b, :])
        mrow = jnp.sum(jnp.where(prow == plane, jnp.concatenate(mc, axis=0), 0.0), axis=0, keepdims=True)
        lrow = jnp.sum(jnp.where(prow == plane, jnp.concatenate(lc, axis=0), 0.0), axis=0, keepdims=True)
        high = lrow.astype(BF16).astype(F32)
        sub = lax.broadcasted_iota(jnp.int32, (16, 128), 0)
        block = jnp.where(sub == 0, mrow, jnp.where(sub == 1, high, jnp.where(sub == 2, lrow - high, 0.0)))
        dst[at, lanes:lanes + 16, :] = block.astype(BF16)

    def send(k):
        o_copy(chip_from(k), chip).start()

    def run(first_k, count, side, top, body):
        def two(i, top):
            k = first_k + 2 * i
            return body(k + 1, 1 - side, body(k, side, top))

        pairs = (count - 1) // 2
        top = lax.fori_loop(0, pairs, two, top)
        for k in range(2 * pairs, count):
            top = body(first_k + k, side, top, k == count - 1)
            side = 1 - side
        return side, top

    loads[4].wait()
    q_copy(0, 1).wait_recv()
    for g in range(groups):
        for i in range(2):
            kv_copy(g, i).wait_recv()
    top = advance(None, tile_of(0), 1, None)

    def before(k, slot, top, last=False):
        if last:
            for j in range(n1, chips):
                q_wait(j)
            then = (bslot[0], 1)
        else:
            q_wait(early[k + 1])
            then = tile_of(early[k + 1])
        top, *res = advance(tile_of(early[k])[1], then, slot, top)
        keep(nb + k, *res)
        return top

    slot = 0
    for k in range(n1):
        top = before(k, slot, top, k == n1 - 1)
        slot = 1 - slot

    for e in range(nb):
        then = (bslot[e + 1], e + 2) if e + 1 < nb else tile_of(late(0))
        top, *res = advance(e + 1, then, slot, top)
        keep(e, *res)
        slot = 1 - slot

    for k in range(n1 - 1, 0, -1):
        finish(early[k], nb + k, sendb, chip_from(early[k]))
        send(early[k])

    finish(0, nb, own_part, 0)

    def after(j, slot, top, last=False):
        k = late(j)
        top, *res = advance(tile_of(k)[1], None if last else tile_of(late(j + 1)), slot, top)
        keep(nb, *res)
        finish(k, nb, sendb, chip_from(k))
        send(k)
        return top

    run(0, chips - n1, slot, top, after)

    x_copy().wait_recv()

    @pl.loop(1, chips)
    def _(j):
        o_copy(chip, (chip + j) % chips).wait_recv()

    def partial(i, part_rows):
        return (recvb[(chip + i) % chips, part_rows, :] if i else own_part[0, part_rows, :]).astype(F32)

    ms, ls = [], []
    for i in range(chips):
        block = partial(i, slice(lanes, lanes + 16))
        ms.append(block[0:1])
        ls.append(block[1:2] + block[2:3])
    for block in (sfx[core, half:half + 8, :], sfx_in[half:half + 8, :]):
        ms.append(block[0:1])
        ls.append(block[1:2])
    peak = functools.reduce(jnp.maximum, ms)
    ws = [jnp.exp2(m - peak) for m in ms]
    inv = 1.0 / sum(a * b for a, b in zip(ws, ls))
    coef[...] = jnp.zeros_like(coef)
    for i, a in enumerate(ws):
        coef[i:i + 1, :] = a * inv
    ct = coef[...].T
    acc = jnp.zeros((lanes, hd), F32)
    for i in range(chips):
        acc += ct[:, i:i + 1] * partial(i, slice(0, lanes))
    mo = pl.ds(pl.multiple_of(core * half, half), half)
    so = pl.ds(pl.multiple_of(other * half, half), half)
    fin[mo, :] = acc[:half] + ct[:half, chips:chips + 1] * sfx[core, :half, :]
    fin[so, :] = acc[half:] + ct[half:, chips + 1:chips + 2] * sfx_in[:half, :]
    for h in range(per_kv):
        attn_all[0, :, h * hd:(h + 1) * hd] = fin[pl.ds(h, 2 * rows, stride=per_kv), :].astype(BF16)

    def a_copy(k):
        return to_page(attn_all.at[0], attn_all.at[k], a_ss.at[k], a_rs.at[k], chip_to(k) * 2 + core)

    for k in far_first:
        a_copy(k).start()

    q_copy(0, 1).wait_send()
    for k in range(1, chips):
        q_copy(k, 0).wait_send()
        q_copy(k, 1).wait_send()
    for g in range(groups):
        for i in range(2):
            kv_copy(g, i).wait_send()
    w_copy().wait_send()
    x_copy().wait_send()

    @pl.loop(1, chips)
    def _(j):
        o_copy((chip + j) % chips, chip).wait_send()

    loads[3].wait()
    w_copy().wait_recv()
    zrows = out.shape[0]
    pin[z * 2 + core] = jnp.zeros(pin.shape[1:], BF16)

    def p_copy(dst_z, dst_core, src_z, src_core):
        return pltpu.make_async_remote_copy(
            src_ref=part.at[dst_z * 2 + dst_core], dst_ref=pin.at[src_z * 2 + src_core],
            send_sem=p_ss.at[dst_z * 2 + dst_core], recv_sem=p_rs.at[src_z * 2 + src_core],
            device_id={"kvh": dst_z, "page": chip * 2 + dst_core}, device_id_type=MESH)

    for k in range(1, chips):
        a_copy(k).wait_recv()
    for k in range(chips):
        at = chip_from(k) * (2 * rows)
        a_f32[pl.ds(pl.multiple_of(at, 2 * rows), 2 * rows), :] = attn_all[k].astype(F32)
    a = a_f32[...].astype(BF16)
    y = jnp.dot(a, wr[...], preferred_element_type=F32)
    for k in range(zs):
        part[k * 2 + other] = y[k * zrows:(k + 1) * zrows].astype(BF16)

    @pl.loop(0, zs)
    def _(j):
        p_copy((z + j) % zs, other, z, core).start()

    y = jnp.dot(a, wl[...], preferred_element_type=F32)
    pf[...] = y
    for k in range(zs):
        part[k * 2 + core] = y[k * zrows:(k + 1) * zrows].astype(BF16)

    @pl.loop(1, zs)
    def _(j):
        p_copy((z + j) % zs, core, z, core).start()

    for k in range(1, chips):
        a_copy(k).wait_send()

    @pl.loop(0, zs)
    def _(j):
        p_copy(z, core, (z + j) % zs, other).wait_recv()

    @pl.loop(1, zs)
    def _(j):
        p_copy(z, core, (z + j) % zs, core).wait_recv()

    total = pf[pl.ds(pl.multiple_of(z * zrows, zrows), zrows), :]
    for i in range(2 * zs):
        total += pin[i].astype(F32)
    out[...] = total.astype(BF16)

    @pl.loop(0, zs)
    def _(j):
        p_copy((z + j) % zs, other, z, core).wait_send()

    @pl.loop(1, zs)
    def _(j):
        p_copy((z + j) % zs, core, z, core).wait_send()


def on_device(pages, zs, queries, gid, slen, tab, pk, pv, sk, sv, w):
    rows, heads, hd = queries.shape
    groups, tokens, kvs = pk.shape[:3]
    per_kv = heads // kvs
    pool, plen = sk.shape[:2]
    sufp = tab.shape[1]
    chips = pages // 2
    side = math.isqrt(chips)
    side = side if side * side == chips else 1
    lanes = 2 * rows * per_kv
    half = rows * per_kv
    kept = groups - 1 + chips // side
    feats, cols = w.shape
    fh = feats // 2
    zrows = rows * pages // zs
    pk = pk.reshape(groups, tokens * kvs, hd)
    pv = pv.reshape(groups, tokens * kvs, hd)
    sk = sk.reshape(pool, plen * kvs, hd)
    sv = sv.reshape(pool, plen * kvs, hd)
    V, D = pltpu.VMEM, pltpu.SemaphoreType.DMA
    smem = pl.BlockSpec(memory_space=pltpu.SMEM)
    anym = pl.BlockSpec(memory_space=pl.ANY)
    scratch = [
        V((rows, heads, hd), BF16), V((chips, 2, rows, per_kv, hd), BF16),
        V((groups, 2 * tokens, hd), BF16), V((groups, 2 * tokens, hd), BF16), V((2 * tokens, hd), F32),
        V((groups, 2, tokens, hd), BF16), V((groups, 2, tokens, hd), BF16),
        V((groups, tokens, hd), BF16), V((groups, tokens, hd), BF16),
        V((pool, plen * kvs, hd), BF16), V((pool, plen * kvs, hd), BF16),
        V((fh, cols), BF16), V((fh, cols), BF16), V((2, lanes, 2 * tokens), F32),
        V((kept, lanes, hd), F32), V((kept, lanes, 128), F32), V((kept, lanes, 128), F32),
        V((chips, lanes + 16, hd), BF16), V((chips, lanes + 16, hd), BF16), V((1, lanes + 16, hd), BF16),
        V((2, half + 8, hd), F32), V((half + 8, hd), F32), V((2, half, 128), F32), V((2, half, 128), F32),
        V((128, 128), F32), V((lanes, hd), F32), V((chips, 2 * rows, fh), BF16), V((rows * pages, fh), F32),
        V((rows * pages, cols), F32), V((2 * zs, zrows, cols), BF16), V((2 * zs, zrows, cols), BF16),
        D((6 + 2 * groups,)), D((pages,)), D((pages,)), D((2 * groups,)), D((2 * groups,)), D, D, D, D,
        D((chips,)), D((chips,)), D((chips,)), D((chips,)), D((2 * zs,)), D((2 * zs,)),
    ]
    dims = (rows, per_kv, hd, tokens, groups, sufp)
    return pl.pallas_call(
        functools.partial(kernel, pages, zs, (side, chips // side), dims),
        out_shape=jax.ShapeDtypeStruct((zrows, cols), BF16),
        in_specs=[smem] * 3 + [anym] * 6,
        out_specs=pl.BlockSpec(memory_space=pltpu.VMEM),
        scratch_shapes=scratch,
        compiler_params=pltpu.CompilerParams(
            collective_id=0, has_side_effects=True, vmem_limit_bytes=56 * 1024 * 1024),
    )(gid, slen, tab, queries, pk, pv, sk, sv, w)


def solution(mesh):
    placed = (
        P("page", "kvh", None), P(), P("page"), P("page", None),
        P(None, "page", "kvh", None), P(None, "page", "kvh", None),
        P("page", None, "kvh", None), P("page", None, "kvh", None), P("kvh", "page"),
    )
    return jax.shard_map(
        functools.partial(on_device, mesh.shape["page"], mesh.shape["kvh"]),
        mesh=mesh, in_specs=placed, out_specs=P("kvh", "page"), check_vma=False)
```

```python
import functools
import math

import jax
import jax.numpy as jnp
from jax import lax
from jax.experimental import pallas as pl
from jax.experimental.pallas import tpu as pltpu
from jax.sharding import PartitionSpec as P

MESH = pl.DeviceIdType.MESH
F32 = jnp.float32
BF16 = jnp.bfloat16
LOW = -1e30


def nt_dot(a, b):
    return lax.dot_general(a, b, (((1,), (1,)), ((), ())), preferred_element_type=F32)


def kernel(
    pages, zs, sides, dims,
    gid_in, slen_in, tab_in, q_in, pk, pv, sk, sv, w_in, out,
    gid, slen, tab, qv, q_all, kraw, vraw, stage, kd, vd, kr, vr, skv, svv, wl, wr, s_ref,
    acc_s, m_s, l_s, sendb, recvb, own_part, sfx, sfx_in, smc, slc, coef, fin, attn_all, a_mat, pf, part, pin,
    loc, q_ss, q_rs, kv_ss, kv_rs, w_ss, w_rs, x_ss, x_rs, o_ss, o_rs, a_ss, a_rs, p_ss, p_rs,
):
    rows, per_kv, hd, tokens, groups, sufp = dims
    chips = pages // 2
    lanes = 2 * rows * per_kv
    c2 = hd ** (-0.5) * math.log2(math.e)
    me = lax.axis_index("page")
    z = lax.axis_index("kvh")
    chip = me // 2
    core = me % 2
    other = 1 - core
    sib = chip * 2 + other
    sx, sy = sides
    cx, cy = chip // sy, chip % sy
    far_first = sorted(range(1, chips), key=lambda k: -min(k // sy, sx - k // sy) - min(k % sy, sy - k % sy))

    def chip_at(dx, dy):
        return (cx + dx) % sx * sy + (cy + dy) % sy

    def peer(j):
        k = jnp.int32(0)
        for i, v in enumerate(far_first):
            k = jnp.where(j == i, v, k)
        return chip_at(k // sy, k % sy)

    def to_page(src, dst, ss, rs, page):
        return pltpu.make_async_remote_copy(
            src_ref=src, dst_ref=dst, send_sem=ss, recv_sem=rs,
            device_id={"page": page}, device_id_type=MESH)

    bar = pltpu.get_barrier_semaphore()

    @pl.loop(1, pages)
    def _(j):
        pl.semaphore_signal(bar, inc=1, device_id={"page": (me + j) % pages}, device_id_type=MESH)

    @pl.loop(1, zs)
    def _(j):
        for cc in range(2):
            pl.semaphore_signal(
                bar, inc=1, device_id={"kvh": (z + j) % zs, "page": chip * 2 + cc}, device_id_type=MESH)

    loads = [
        pltpu.make_async_copy(q_in, qv, loc.at[0]),
        pltpu.make_async_copy(sk, skv, loc.at[1]),
        pltpu.make_async_copy(sv, svv, loc.at[2]),
        pltpu.make_async_copy(w_in.at[pl.ds(core * wl.shape[0], wl.shape[0])], wl, loc.at[3]),
        pltpu.make_async_copy(q_in.at[:, pl.ds(core * per_kv, per_kv)], q_all.at[chip, core], loc.at[4]),
    ]
    kvl = []
    for g in range(groups):
        kvl.append(pltpu.make_async_copy(pk.at[g], kraw.at[g], loc.at[6 + 2 * g]))
        kvl.append(pltpu.make_async_copy(pv.at[g], vraw.at[g], loc.at[7 + 2 * g]))
    small = [
        pltpu.make_async_copy(src, dst, loc.at[6 + 2 * groups + i])
        for i, (src, dst) in enumerate(((gid_in, gid), (slen_in, slen), (tab_in, tab)))]
    for copy in small + [loads[0], loads[4]] + kvl + loads[1:4]:
        copy.start()

    pl.semaphore_wait(bar, pages - 1 + 2 * (zs - 1))

    def q_copy(page, src_page):
        kv = page % 2
        return to_page(
            q_in.at[:, pl.ds(kv * per_kv, per_kv)], q_all.at[src_page // 2, src_page % 2],
            q_ss.at[page], q_rs.at[src_page], page)

    for k in far_first:
        for cc in range(2):
            q_copy(chip_at(k // sy, k % sy) * 2 + cc, me).start()
    q_copy(sib, me).start()

    for copy in small:
        copy.wait()

    def count(r, c):
        g = gid[r]
        return tuple(c[e] + (g <= e).astype(jnp.int32) for e in range(groups - 1))

    first = lax.fori_loop(0, rows * pages, count, (jnp.int32(0),) * (groups - 1))
    btile = [jnp.minimum(f // (2 * rows), chips - 1) for f in first]

    def kv_copy(g, i):
        return to_page((kd, vd)[i].at[g, other], (kr, vr)[i].at[g], kv_ss.at[2 * g + i], kv_rs.at[2 * g + i], sib)

    for g in range(groups):
        for i in range(2):
            kvl[2 * g + i].wait()
            stage[...] = (kraw, vraw)[i][g].astype(F32)
            for kv in range(2):
                (kd, vd)[i][g, kv] = stage[pl.ds(kv, tokens, stride=2), :].astype(BF16)
            kv_copy(g, i).start()

    def w_copy():
        return to_page(w_in.at[pl.ds(other * wl.shape[0], wl.shape[0])], wr, w_ss, w_rs, sib)

    span = sufp * skv.shape[1]
    both = 2 * per_kv
    col = lax.broadcasted_iota(jnp.int32, (both, span), 1)
    row = lax.broadcasted_iota(jnp.int32, (both, span), 0)
    mine = (col % 2) == (row // per_kv)
    token = col // 2
    for copy in loads[:3]:
        copy.wait()
    for r in range(rows):
        pgs = [tab[r, j] % skv.shape[0] for j in range(sufp)]
        keys = jnp.concatenate([skv[pg] for pg in pgs], axis=0)
        vals = jnp.concatenate([svv[pg] for pg in pgs], axis=0)
        live = mine & (token < slen[r])
        s = jnp.where(live, nt_dot(qv[r], keys) * c2, LOW)
        top = jnp.max(s, axis=1, keepdims=True)
        p = jnp.where(live, jnp.exp2(s - top), 0.0)
        tot = jnp.sum(p, axis=1, keepdims=True)
        o = jnp.dot(p.astype(BF16), vals, preferred_element_type=F32)
        for kv in range(2):
            a, b = kv * per_kv, (kv + 1) * per_kv
            sfx[kv, r * per_kv:(r + 1) * per_kv, :] = o[a:b]
            smc[kv, r * per_kv:(r + 1) * per_kv, :] = jnp.broadcast_to(top[a:b], (per_kv, 128))
            slc[kv, r * per_kv:(r + 1) * per_kv, :] = jnp.broadcast_to(tot[a:b], (per_kv, 128))
    half = rows * per_kv
    hrow = lax.broadcasted_iota(jnp.int32, (half, 128), 0) + core * half
    hlane = lax.broadcasted_iota(jnp.int32, (half, 128), 1)
    sub8 = lax.broadcasted_iota(jnp.int32, (8, 128), 0)
    lane8 = lax.broadcasted_iota(jnp.int32, (8, 128), 1)
    held = (lane8 // half) == core
    for kv in range(2):
        mrow = jnp.sum(jnp.where(hrow == hlane, smc[kv], 0.0), axis=0, keepdims=True)
        lrow = jnp.sum(jnp.where(hrow == hlane, slc[kv], 0.0), axis=0, keepdims=True)
        block = jnp.where(sub8 == 0, mrow, jnp.where(sub8 == 1, lrow, 0.0))
        sfx[kv, half:half + 8, :] = jnp.where(held, block, jnp.where(sub8 == 0, LOW, 0.0))

    def x_copy():
        return to_page(sfx.at[other], sfx_in, x_ss, x_rs, sib)

    x_copy().start()

    loads[4].wait()

    @pl.loop(1, pages)
    def _(j):
        q_copy(me, (me + j) % pages).wait_recv()

    for g in range(groups):
        for i in range(2):
            kv_copy(g, i).wait_recv()

    w_copy().start()

    def o_copy(dst_chip, src_chip):
        return to_page(sendb.at[dst_chip], recvb.at[src_chip], o_ss.at[dst_chip], o_rs.at[src_chip], dst_chip * 2 + core)

    prow = lax.broadcasted_iota(jnp.int32, (lanes, 128), 0)
    plane = lax.broadcasted_iota(jnp.int32, (lanes, 128), 1)
    nb = groups - 1

    def tile_of(k):
        t = peer(k)
        return t, gid[t * (2 * rows)]

    def columns(f, x):
        return functools.reduce(f, [x[:, i * 128:(i + 1) * 128] for i in range(tokens // 128)] if tokens > 128 else [x])

    def advance(now, then, slot, top_in):
        if now is not None:
            top = (jnp.max(top_in, axis=1, keepdims=True) * c2).astype(BF16).astype(F32)
        if then is not None:
            q = q_all[then[0]].reshape(lanes, hd)
        o, tot, top_out = None, None, None
        for i in range(2):
            part_of = slice(i * tokens, (i + 1) * tokens)
            if then is not None:
                x = nt_dot(q, kr[then[1]] if i else kd[then[1], core])
                s_ref[1 - slot, :, part_of] = x
                m = columns(jnp.maximum, x)
                top_out = m if i == 0 else jnp.maximum(top_out, m)
            if now is not None:
                p = jnp.exp2(s_ref[slot, :, part_of] * c2 - top)
                l = columns(jnp.add, p)
                tot = l if i == 0 else tot + l
                d = jnp.dot(p.astype(BF16), vr[now] if i else vd[now, core], preferred_element_type=F32)
                o = d if i == 0 else o + d
        if now is None:
            return top_out
        return top_out, o, top, jnp.sum(tot, axis=1, keepdims=True)

    def keep(at, o, top, tot):
        acc_s[at] = o
        m_s[at] = jnp.broadcast_to(top, (lanes, 128))
        l_s[at] = jnp.broadcast_to(tot, (lanes, 128))

    def finish(k, dst, at):
        t, g_low = tile_of(k)
        mc, lc = [], []
        for r in range(2 * rows):
            g_r = gid[t * (2 * rows) + r]
            src = jnp.where(g_r == g_low, nb, jnp.maximum(g_r - 1, 0))
            a, b = r * per_kv, (r + 1) * per_kv
            dst[at, a:b, :] = acc_s[src, a:b, :].astype(BF16)
            mc.append(m_s[src, a:b, :])
            lc.append(l_s[src, a:b, :])
        mrow = jnp.sum(jnp.where(prow == plane, jnp.concatenate(mc, axis=0), 0.0), axis=0, keepdims=True)
        lrow = jnp.sum(jnp.where(prow == plane, jnp.concatenate(lc, axis=0), 0.0), axis=0, keepdims=True)
        high = lrow.astype(BF16).astype(F32)
        sub = lax.broadcasted_iota(jnp.int32, (16, 128), 0)
        block = jnp.where(sub == 0, mrow, jnp.where(sub == 1, high, jnp.where(sub == 2, lrow - high, 0.0)))
        dst[at, lanes:lanes + 16, :] = block.astype(BF16)

    top = advance(None, (btile[0], 1), 1, None)
    for e in range(nb):
        then = (btile[e + 1], e + 2) if e + 1 < nb else tile_of(0)
        top, *res = advance(e + 1, then, e % 2, top)
        keep(e, *res)
    base = nb % 2

    def one(k, slot, top, last=False):
        t, g = tile_of(k)
        top, *res = advance(g, None if last else tile_of(k + 1), slot, top)
        keep(nb, *res)
        if last:
            finish(k, own_part, 0)
        else:
            finish(k, sendb, t)
            o_copy(t, chip).start()
        return top

    def pair(i, top):
        return one(2 * i + 1, 1 - base, one(2 * i, base, top))

    top = lax.fori_loop(0, chips // 2 - 1, pair, top)
    top = one(chips - 2, base, top)
    one(chips - 1, 1 - base, top, last=True)

    x_copy().wait_recv()

    @pl.loop(1, chips)
    def _(j):
        o_copy(chip, (chip + j) % chips).wait_recv()

    def partial(i, part_rows):
        return (recvb[(chip + i) % chips, part_rows, :] if i else own_part[0, part_rows, :]).astype(F32)

    ms, ls = [], []
    for i in range(chips):
        block = partial(i, slice(lanes, lanes + 16))
        ms.append(block[0:1])
        ls.append(block[1:2] + block[2:3])
    for block in (sfx[core, half:half + 8, :], sfx_in[half:half + 8, :]):
        ms.append(block[0:1])
        ls.append(block[1:2])
    peak = functools.reduce(jnp.maximum, ms)
    ws = [jnp.exp2(m - peak) for m in ms]
    inv = 1.0 / sum(a * b for a, b in zip(ws, ls))
    coef[...] = jnp.zeros_like(coef)
    for i, a in enumerate(ws):
        coef[i:i + 1, :] = a * inv
    ct = coef[...].T
    acc = jnp.zeros((lanes, hd), F32)
    for i in range(chips):
        acc += ct[:, i:i + 1] * partial(i, slice(0, lanes))
    fin[...] = acc
    mo = pl.ds(pl.multiple_of(core * half, half), half)
    so = pl.ds(pl.multiple_of(other * half, half), half)
    smc[0] = jnp.where(core == 0, ct[:half, chips:chips + 1], ct[half:, chips:chips + 1]) * sfx[core, :half, :]
    smc[1] = jnp.where(core == 0, ct[half:, chips + 1:chips + 2], ct[:half, chips + 1:chips + 2]) * sfx_in[:half, :]
    fin[mo, :] += smc[0]
    fin[so, :] += smc[1]
    for h in range(per_kv):
        attn_all[chip, :, h * hd:(h + 1) * hd] = fin[pl.ds(h, 2 * rows, stride=per_kv), :].astype(BF16)

    def a_copy(dst_chip, src_chip):
        return to_page(
            attn_all.at[src_chip], attn_all.at[src_chip], a_ss.at[dst_chip], a_rs.at[src_chip], dst_chip * 2 + core)

    for k in far_first:
        a_copy(chip_at(k // sy, k % sy), chip).start()

    @pl.loop(1, pages)
    def _(j):
        q_copy((me + j) % pages, me).wait_send()

    for g in range(groups):
        for i in range(2):
            kv_copy(g, i).wait_send()
    w_copy().wait_send()
    x_copy().wait_send()

    @pl.loop(1, chips)
    def _(j):
        o_copy((chip + j) % chips, chip).wait_send()

    loads[3].wait()
    w_copy().wait_recv()
    zrows = out.shape[0]
    pin[z * 2 + core] = jnp.zeros(pin.shape[1:], BF16)

    @pl.loop(1, chips)
    def _(j):
        a_copy(chip, (chip + j) % chips).wait_recv()

    for i in range(chips // 2):
        pair = jnp.concatenate([attn_all[2 * i].astype(F32), attn_all[2 * i + 1].astype(F32)], axis=0)
        a_mat[i * 4 * rows:(i + 1) * 4 * rows, :] = pair.astype(BF16)

    def p_copy(dst_z, dst_core, src_z, src_core):
        return pltpu.make_async_remote_copy(
            src_ref=part.at[dst_z * 2 + dst_core], dst_ref=pin.at[src_z * 2 + src_core],
            send_sem=p_ss.at[dst_z * 2 + dst_core], recv_sem=p_rs.at[src_z * 2 + src_core],
            device_id={"kvh": dst_z, "page": chip * 2 + dst_core}, device_id_type=MESH)

    y = jnp.dot(a_mat[...], wr[...], preferred_element_type=F32)
    for k in range(zs):
        part[k * 2 + other] = y[k * zrows:(k + 1) * zrows].astype(BF16)

    @pl.loop(0, zs)
    def _(j):
        p_copy((z + j) % zs, other, z, core).start()

    y = jnp.dot(a_mat[...], wl[...], preferred_element_type=F32)
    pf[...] = y
    for k in range(zs):
        part[k * 2 + core] = y[k * zrows:(k + 1) * zrows].astype(BF16)

    @pl.loop(1, zs)
    def _(j):
        p_copy((z + j) % zs, core, z, core).start()

    @pl.loop(1, chips)
    def _(j):
        a_copy((chip + j) % chips, chip).wait_send()

    @pl.loop(0, zs)
    def _(j):
        p_copy(z, core, (z + j) % zs, other).wait_recv()

    @pl.loop(1, zs)
    def _(j):
        p_copy(z, core, (z + j) % zs, core).wait_recv()

    total = pf[pl.ds(pl.multiple_of(z * zrows, zrows), zrows), :]
    for i in range(2 * zs):
        total += pin[i].astype(F32)
    out[...] = total.astype(BF16)

    @pl.loop(0, zs)
    def _(j):
        p_copy((z + j) % zs, other, z, core).wait_send()

    @pl.loop(1, zs)
    def _(j):
        p_copy((z + j) % zs, core, z, core).wait_send()


def on_device(pages, zs, queries, gid, slen, tab, pk, pv, sk, sv, w):
    rows, heads, hd = queries.shape
    groups, tokens, kvs = pk.shape[:3]
    per_kv = heads // kvs
    pool, plen = sk.shape[:2]
    sufp = tab.shape[1]
    chips = pages // 2
    side = math.isqrt(chips)
    side = side if side * side == chips else 1
    lanes = 2 * rows * per_kv
    half = rows * per_kv
    feats, cols = w.shape
    fh = feats // 2
    zrows = rows * pages // zs
    pk = pk.reshape(groups, tokens * kvs, hd)
    pv = pv.reshape(groups, tokens * kvs, hd)
    sk = sk.reshape(pool, plen * kvs, hd)
    sv = sv.reshape(pool, plen * kvs, hd)
    V, D = pltpu.VMEM, pltpu.SemaphoreType.DMA
    anym = pl.BlockSpec(memory_space=pl.ANY)
    scratch = [
        pltpu.SMEM(gid.shape, jnp.int32), pltpu.SMEM(slen.shape, jnp.int32), pltpu.SMEM(tab.shape, jnp.int32),
        V((rows, heads, hd), BF16), V((chips, 2, rows, per_kv, hd), BF16),
        V((groups, 2 * tokens, hd), BF16), V((groups, 2 * tokens, hd), BF16), V((2 * tokens, hd), F32),
        V((groups, 2, tokens, hd), BF16), V((groups, 2, tokens, hd), BF16),
        V((groups, tokens, hd), BF16), V((groups, tokens, hd), BF16),
        V((pool, plen * kvs, hd), BF16), V((pool, plen * kvs, hd), BF16),
        V((fh, cols), BF16), V((fh, cols), BF16), V((2, lanes, 2 * tokens), F32),
        V((groups, lanes, hd), F32), V((groups, lanes, 128), F32), V((groups, lanes, 128), F32),
        V((chips, lanes + 16, hd), BF16), V((chips, lanes + 16, hd), BF16), V((1, lanes + 16, hd), BF16),
        V((2, half + 8, hd), F32), V((half + 8, hd), F32), V((2, half, 128), F32), V((2, half, 128), F32),
        V((128, 128), F32), V((lanes, hd), F32), V((chips, 2 * rows, fh), BF16), V((rows * pages, fh), BF16),
        V((rows * pages, cols), F32), V((2 * zs, zrows, cols), BF16), V((2 * zs, zrows, cols), BF16),
        D((9 + 2 * groups,)), D((pages,)), D((pages,)), D((2 * groups,)), D((2 * groups,)), D, D, D, D,
        D((chips,)), D((chips,)), D((chips,)), D((chips,)), D((2 * zs,)), D((2 * zs,)),
    ]
    dims = (rows, per_kv, hd, tokens, groups, sufp)
    return pl.pallas_call(
        functools.partial(kernel, pages, zs, (side, chips // side), dims),
        out_shape=jax.ShapeDtypeStruct((zrows, cols), BF16),
        in_specs=[anym] * 9,
        out_specs=pl.BlockSpec(memory_space=pltpu.VMEM),
        scratch_shapes=scratch,
        compiler_params=pltpu.CompilerParams(
            collective_id=0, has_side_effects=True, vmem_limit_bytes=56 * 1024 * 1024),
    )(gid, slen, tab, queries, pk, pv, sk, sv, w)


def solution(mesh):
    placed = (
        P("page", "kvh", None), P(), P("page"), P("page", None),
        P(None, "page", "kvh", None), P(None, "page", "kvh", None),
        P("page", None, "kvh", None), P("page", None, "kvh", None), P("kvh", "page"),
    )
    return jax.shard_map(
        functools.partial(on_device, mesh.shape["page"], mesh.shape["kvh"]),
        mesh=mesh, in_specs=placed, out_specs=P("kvh", "page"), check_vma=False)
```

```python
import functools
import math

import jax
import jax.numpy as jnp
from jax import lax
from jax.experimental import pallas as pl
from jax.experimental.pallas import tpu as pltpu
from jax.sharding import PartitionSpec as P

MESH = pl.DeviceIdType.MESH
F32 = jnp.float32
BF16 = jnp.bfloat16
LOW = -1e30


def nt_dot(a, b):
    return lax.dot_general(a, b, (((1,), (1,)), ((), ())), preferred_element_type=F32)


def kernel(
    pages, zs, sides, dims,
    gid_in, slen_in, tab_in, q_in, pk, pv, sk, sv, w_in, out,
    gid, slen, tab, qv, q_all, kraw, vraw, stage, kd, vd, kr, vr, skv, svv, wl, wr, s_ref,
    acc_s, m_s, l_s, sendb, recvb, own_part, sfx, sfx_in, smc, slc, coef, fin, attn_all, a_f32, pf, part, pin,
    loc, q_ss, q_rs, kv_ss, kv_rs, w_ss, w_rs, x_ss, x_rs, o_ss, o_rs, a_ss, a_rs, p_ss, p_rs,
):
    rows, per_kv, hd, tokens, groups, sufp = dims
    chips = pages // 2
    lanes = 2 * rows * per_kv
    c2 = hd ** (-0.5) * math.log2(math.e)
    me = lax.axis_index("page")
    z = lax.axis_index("kvh")
    chip = me // 2
    core = me % 2
    other = 1 - core
    sib = chip * 2 + other

    sx, sy = sides
    n1 = sy
    cx, cy = chip // sy, chip % sy

    far_first = sorted(range(1, chips), key=lambda k: -min(k // sy, sx - k // sy) - min(k % sy, sy - k % sy))

    def chip_to(k):
        return (cx + k // sy) % sx * sy + (cy + k % sy) % sy

    def chip_from(k):
        return (cx + sx - k // sy) % sx * sy + (cy + sy - k % sy) % sy

    def to_page(src, dst, ss, rs, page):
        return pltpu.make_async_remote_copy(
            src_ref=src, dst_ref=dst, send_sem=ss, recv_sem=rs,
            device_id={"page": page}, device_id_type=MESH)

    bar = pltpu.get_barrier_semaphore()

    @pl.loop(1, pages)
    def _(j):
        pl.semaphore_signal(bar, inc=1, device_id={"page": (me + j) % pages}, device_id_type=MESH)

    @pl.loop(1, zs)
    def _(j):
        for cc in range(2):
            pl.semaphore_signal(
                bar, inc=1, device_id={"kvh": (z + j) % zs, "page": chip * 2 + cc}, device_id_type=MESH)

    loads = [
        pltpu.make_async_copy(q_in, qv, loc.at[0]),
        pltpu.make_async_copy(sk, skv, loc.at[1]),
        pltpu.make_async_copy(sv, svv, loc.at[2]),
        pltpu.make_async_copy(w_in.at[pl.ds(core * wl.shape[0], wl.shape[0])], wl, loc.at[3]),
        pltpu.make_async_copy(q_in.at[:, pl.ds(core * per_kv, per_kv)], q_all.at[0, 0], loc.at[4]),
    ]
    kvl = []
    for g in range(groups):
        kvl.append(pltpu.make_async_copy(pk.at[g], kraw.at[g], loc.at[6 + 2 * g]))
        kvl.append(pltpu.make_async_copy(pv.at[g], vraw.at[g], loc.at[7 + 2 * g]))
    small = [
        pltpu.make_async_copy(src, dst, loc.at[6 + 2 * groups + i])
        for i, (src, dst) in enumerate(((gid_in, gid), (slen_in, slen), (tab_in, tab)))]
    for copy in small + [loads[0], loads[4]] + kvl + loads[1:4]:
        copy.start()

    def kv_copy(g, i):
        return to_page((kd, vd)[i].at[g, other], (kr, vr)[i].at[g], kv_ss.at[2 * g + i], kv_rs.at[2 * g + i], sib)

    for g in range(groups):
        for i in range(2):
            kvl[2 * g + i].wait()
            stage[...] = (kraw, vraw)[i][g].astype(F32)
            for kv in range(2):
                (kd, vd)[i][g, kv] = stage[pl.ds(kv, tokens, stride=2), :].astype(BF16)

    pl.semaphore_wait(bar, pages - 1 + 2 * (zs - 1))

    def q_copy(k, rc):
        kv = other if rc else core
        return to_page(
            q_in.at[:, pl.ds(kv * per_kv, per_kv)], q_all.at[k, rc],
            q_ss.at[2 * k + rc], q_rs.at[2 * k + rc], chip_to(k) * 2 + kv)

    for k in far_first:
        q_copy(k, 0).start()
        q_copy(k, 1).start()
    q_copy(0, 1).start()

    for copy in small:
        copy.wait()

    def count(r, c):
        g = gid[r]
        return tuple(c[e] + (g <= e).astype(jnp.int32) for e in range(groups - 1))

    first = lax.fori_loop(0, rows * pages, count, (jnp.int32(0),) * (groups - 1))
    btile = [jnp.minimum(f // (2 * rows), chips - 1) for f in first]
    bslot = [(cx + sx - b // sy) % sx * sy + (cy + sy - b % sy) % sy for b in btile]

    for g in range(groups):
        for i in range(2):
            kv_copy(g, i).start()

    def w_copy():
        return to_page(w_in.at[pl.ds(other * wl.shape[0], wl.shape[0])], wr, w_ss, w_rs, sib)

    span = sufp * skv.shape[1]
    both = 2 * per_kv
    col = lax.broadcasted_iota(jnp.int32, (both, span), 1)
    row = lax.broadcasted_iota(jnp.int32, (both, span), 0)
    mine = (col % 2) == (row // per_kv)
    token = col // 2
    for copy in loads[:3]:
        copy.wait()
    for r in range(rows):
        pgs = [tab[r, j] % skv.shape[0] for j in range(sufp)]
        keys = jnp.concatenate([skv[pg] for pg in pgs], axis=0)
        vals = jnp.concatenate([svv[pg] for pg in pgs], axis=0)
        live = mine & (token < slen[r])
        s = jnp.where(live, nt_dot(qv[r], keys) * c2, LOW)
        top = jnp.max(s, axis=1, keepdims=True)
        p = jnp.where(live, jnp.exp2(s - top), 0.0)
        tot = jnp.sum(p, axis=1, keepdims=True)
        o = jnp.dot(p.astype(BF16), vals, preferred_element_type=F32)
        for kv in range(2):
            a, b = kv * per_kv, (kv + 1) * per_kv
            sfx[kv, r * per_kv:(r + 1) * per_kv, :] = o[a:b]
            smc[kv, r * per_kv:(r + 1) * per_kv, :] = jnp.broadcast_to(top[a:b], (per_kv, 128))
            slc[kv, r * per_kv:(r + 1) * per_kv, :] = jnp.broadcast_to(tot[a:b], (per_kv, 128))
    half = rows * per_kv
    hrow = lax.broadcasted_iota(jnp.int32, (half, 128), 0)
    hlane = lax.broadcasted_iota(jnp.int32, (half, 128), 1)
    sub8 = lax.broadcasted_iota(jnp.int32, (8, 128), 0)
    lane8 = lax.broadcasted_iota(jnp.int32, (8, 128), 1)
    for kv in range(2):
        side = jnp.where(core == kv, 0, 1)
        held = (lane8 // half) == side
        diag = hlane == hrow + side * half
        mrow = jnp.sum(jnp.where(diag, smc[kv], 0.0), axis=0, keepdims=True)
        lrow = jnp.sum(jnp.where(diag, slc[kv], 0.0), axis=0, keepdims=True)
        block = jnp.where(sub8 == 0, mrow, jnp.where(sub8 == 1, lrow, 0.0))
        sfx[kv, half:half + 8, :] = jnp.where(held, block, jnp.where(sub8 == 0, LOW, 0.0))

    def x_copy():
        return to_page(sfx.at[other], sfx_in, x_ss, x_rs, sib)

    x_copy().start()

    def o_copy(dst_chip, src_chip):
        return to_page(sendb.at[dst_chip], recvb.at[src_chip], o_ss.at[dst_chip], o_rs.at[src_chip], dst_chip * 2 + core)

    prow = lax.broadcasted_iota(jnp.int32, (lanes, 128), 0)
    plane = lax.broadcasted_iota(jnp.int32, (lanes, 128), 1)
    nb = groups - 1

    early = sorted(range(sy), key=lambda d: min(d, sy - d))

    def late(j):
        k = jnp.int32(0)
        for i, v in enumerate([v for v in far_first if v not in early]):
            k = jnp.where(j == i, v, k)
        return k

    def tile_of(k):
        return k, gid[chip_from(k) * (2 * rows)]

    def q_wait(k):
        for rc in range(2):
            q_copy(k, rc).wait_recv()

    def columns(f, x):
        return functools.reduce(f, [x[:, i * 128:(i + 1) * 128] for i in range(tokens // 128)] if tokens > 128 else [x])

    def advance(now, then, slot, top_in):
        if now is not None:
            top = (jnp.max(top_in, axis=1, keepdims=True) * c2).astype(BF16).astype(F32)
        if then is not None:
            q = q_all[then[0]].reshape(lanes, hd)
        o, tot, top_out = None, None, None
        for i in range(2):
            part_of = slice(i * tokens, (i + 1) * tokens)
            if then is not None:
                x = nt_dot(q, kr[then[1]] if i else kd[then[1], core])
                s_ref[1 - slot, :, part_of] = x
                m = columns(jnp.maximum, x)
                top_out = m if i == 0 else jnp.maximum(top_out, m)
            if now is not None:
                p = jnp.exp2(s_ref[slot, :, part_of] * c2 - top)
                l = columns(jnp.add, p)
                tot = l if i == 0 else tot + l
                d = jnp.dot(p.astype(BF16), vr[now] if i else vd[now, core], preferred_element_type=F32)
                o = d if i == 0 else o + d
        if now is None:
            return top_out
        return top_out, o, top, jnp.sum(tot, axis=1, keepdims=True)

    def keep(at, o, top, tot):
        acc_s[at] = o
        m_s[at] = jnp.broadcast_to(top, (lanes, 128))
        l_s[at] = jnp.broadcast_to(tot, (lanes, 128))

    def finish(k, slot, dst, at):
        first_row = chip_from(k) * (2 * rows)
        g_low = gid[first_row]
        mc, lc = [], []
        for r in range(2 * rows):
            g_r = gid[first_row + (core if r < rows else other) * rows + r % rows]
            src = jnp.where(g_r == g_low, slot, jnp.maximum(g_r - 1, 0))
            a, b = r * per_kv, (r + 1) * per_kv
            dst[at, a:b, :] = acc_s[src, a:b, :].astype(BF16)
            mc.append(m_s[src, a:b, :])
            lc.append(l_s[src, a:b, :])
        mrow = jnp.sum(jnp.where(prow == plane, jnp.concatenate(mc, axis=0), 0.0), axis=0, keepdims=True)
        lrow = jnp.sum(jnp.where(prow == plane, jnp.concatenate(lc, axis=0), 0.0), axis=0, keepdims=True)
        high = lrow.astype(BF16).astype(F32)
        sub = lax.broadcasted_iota(jnp.int32, (16, 128), 0)
        block = jnp.where(sub == 0, mrow, jnp.where(sub == 1, high, jnp.where(sub == 2, lrow - high, 0.0)))
        dst[at, lanes:lanes + 16, :] = block.astype(BF16)

    def send(k):
        o_copy(chip_from(k), chip).start()

    def run(first_k, count, side, top, body):
        def two(i, top):
            k = first_k + 2 * i
            return body(k + 1, 1 - side, body(k, side, top))

        pairs = (count - 1) // 2
        top = lax.fori_loop(0, pairs, two, top)
        for k in range(2 * pairs, count):
            top = body(first_k + k, side, top, k == count - 1)
            side = 1 - side
        return side, top

    loads[4].wait()
    q_copy(0, 1).wait_recv()
    for g in range(groups):
        for i in range(2):
            kv_copy(g, i).wait_recv()
    top = advance(None, tile_of(0), 1, None)

    def before(k, slot, top, last=False):
        if last:
            for j in range(n1, chips):
                q_wait(j)
            then = (bslot[0], 1)
        else:
            q_wait(early[k + 1])
            then = tile_of(early[k + 1])
        top, *res = advance(tile_of(early[k])[1], then, slot, top)
        keep(nb + k, *res)
        return top

    slot = 0
    for k in range(n1):
        top = before(k, slot, top, k == n1 - 1)
        slot = 1 - slot

    for e in range(nb):
        then = (bslot[e + 1], e + 2) if e + 1 < nb else tile_of(late(0))
        top, *res = advance(e + 1, then, slot, top)
        keep(e, *res)
        slot = 1 - slot

    w_copy().start()

    for k in range(n1 - 1, 0, -1):
        finish(early[k], nb + k, sendb, chip_from(early[k]))
        send(early[k])

    finish(0, nb, own_part, 0)

    def after(j, slot, top, last=False):
        k = late(j)
        top, *res = advance(tile_of(k)[1], None if last else tile_of(late(j + 1)), slot, top)
        keep(nb, *res)
        finish(k, nb, sendb, chip_from(k))
        send(k)
        return top

    run(0, chips - n1, slot, top, after)

    x_copy().wait_recv()

    @pl.loop(1, chips)
    def _(j):
        o_copy(chip, (chip + j) % chips).wait_recv()

    def partial(i, part_rows):
        return (recvb[(chip + i) % chips, part_rows, :] if i else own_part[0, part_rows, :]).astype(F32)

    ms, ls = [], []
    for i in range(chips):
        block = partial(i, slice(lanes, lanes + 16))
        ms.append(block[0:1])
        ls.append(block[1:2] + block[2:3])
    for block in (sfx[core, half:half + 8, :], sfx_in[half:half + 8, :]):
        ms.append(block[0:1])
        ls.append(block[1:2])
    peak = functools.reduce(jnp.maximum, ms)
    ws = [jnp.exp2(m - peak) for m in ms]
    inv = 1.0 / sum(a * b for a, b in zip(ws, ls))
    coef[...] = jnp.zeros_like(coef)
    for i, a in enumerate(ws):
        coef[i:i + 1, :] = a * inv
    ct = coef[...].T
    acc = jnp.zeros((lanes, hd), F32)
    for i in range(chips):
        acc += ct[:, i:i + 1] * partial(i, slice(0, lanes))
    mo = pl.ds(pl.multiple_of(core * half, half), half)
    so = pl.ds(pl.multiple_of(other * half, half), half)
    fin[mo, :] = acc[:half] + ct[:half, chips:chips + 1] * sfx[core, :half, :]
    fin[so, :] = acc[half:] + ct[half:, chips + 1:chips + 2] * sfx_in[:half, :]
    for h in range(per_kv):
        attn_all[0, :, h * hd:(h + 1) * hd] = fin[pl.ds(h, 2 * rows, stride=per_kv), :].astype(BF16)

    def a_copy(k):
        return to_page(attn_all.at[0], attn_all.at[k], a_ss.at[k], a_rs.at[k], chip_to(k) * 2 + core)

    for k in far_first:
        a_copy(k).start()

    q_copy(0, 1).wait_send()
    for k in range(1, chips):
        q_copy(k, 0).wait_send()
        q_copy(k, 1).wait_send()
    for g in range(groups):
        for i in range(2):
            kv_copy(g, i).wait_send()
    w_copy().wait_send()
    x_copy().wait_send()

    @pl.loop(1, chips)
    def _(j):
        o_copy((chip + j) % chips, chip).wait_send()

    loads[3].wait()
    w_copy().wait_recv()
    zrows = out.shape[0]
    pin[z * 2 + core] = jnp.zeros(pin.shape[1:], BF16)

    def p_copy(dst_z, dst_core, src_z, src_core):
        return pltpu.make_async_remote_copy(
            src_ref=part.at[dst_z * 2 + dst_core], dst_ref=pin.at[src_z * 2 + src_core],
            send_sem=p_ss.at[dst_z * 2 + dst_core], recv_sem=p_rs.at[src_z * 2 + src_core],
            device_id={"kvh": dst_z, "page": chip * 2 + dst_core}, device_id_type=MESH)

    for k in range(1, chips):
        a_copy(k).wait_recv()
    for k in range(chips):
        at = chip_from(k) * (2 * rows)
        a_f32[pl.ds(pl.multiple_of(at, 2 * rows), 2 * rows), :] = attn_all[k].astype(F32)
    a = a_f32[...].astype(BF16)
    y = jnp.dot(a, wr[...], preferred_element_type=F32)
    for k in range(zs):
        part[k * 2 + other] = y[k * zrows:(k + 1) * zrows].astype(BF16)

    @pl.loop(0, zs)
    def _(j):
        p_copy((z + j) % zs, other, z, core).start()

    y = jnp.dot(a, wl[...], preferred_element_type=F32)
    pf[...] = y
    for k in range(zs):
        part[k * 2 + core] = y[k * zrows:(k + 1) * zrows].astype(BF16)

    @pl.loop(1, zs)
    def _(j):
        p_copy((z + j) % zs, core, z, core).start()

    for k in range(1, chips):
        a_copy(k).wait_send()

    @pl.loop(0, zs)
    def _(j):
        p_copy(z, core, (z + j) % zs, other).wait_recv()

    @pl.loop(1, zs)
    def _(j):
        p_copy(z, core, (z + j) % zs, core).wait_recv()

    total = pf[pl.ds(pl.multiple_of(z * zrows, zrows), zrows), :]
    for i in range(2 * zs):
        total += pin[i].astype(F32)
    out[...] = total.astype(BF16)

    @pl.loop(0, zs)
    def _(j):
        p_copy((z + j) % zs, other, z, core).wait_send()

    @pl.loop(1, zs)
    def _(j):
        p_copy((z + j) % zs, core, z, core).wait_send()


def on_device(pages, zs, queries, gid, slen, tab, pk, pv, sk, sv, w):
    rows, heads, hd = queries.shape
    groups, tokens, kvs = pk.shape[:3]
    per_kv = heads // kvs
    pool, plen = sk.shape[:2]
    sufp = tab.shape[1]
    chips = pages // 2
    side = math.isqrt(chips)
    side = side if side * side == chips else 1
    lanes = 2 * rows * per_kv
    half = rows * per_kv
    kept = groups - 1 + chips // side
    feats, cols = w.shape
    fh = feats // 2
    zrows = rows * pages // zs
    pk = pk.reshape(groups, tokens * kvs, hd)
    pv = pv.reshape(groups, tokens * kvs, hd)
    sk = sk.reshape(pool, plen * kvs, hd)
    sv = sv.reshape(pool, plen * kvs, hd)
    V, D = pltpu.VMEM, pltpu.SemaphoreType.DMA
    anym = pl.BlockSpec(memory_space=pl.ANY)
    scratch = [
        pltpu.SMEM(gid.shape, jnp.int32), pltpu.SMEM(slen.shape, jnp.int32), pltpu.SMEM(tab.shape, jnp.int32),
        V((rows, heads, hd), BF16), V((chips, 2, rows, per_kv, hd), BF16),
        V((groups, 2 * tokens, hd), BF16), V((groups, 2 * tokens, hd), BF16), V((2 * tokens, hd), F32),
        V((groups, 2, tokens, hd), BF16), V((groups, 2, tokens, hd), BF16),
        V((groups, tokens, hd), BF16), V((groups, tokens, hd), BF16),
        V((pool, plen * kvs, hd), BF16), V((pool, plen * kvs, hd), BF16),
        V((fh, cols), BF16), V((fh, cols), BF16), V((2, lanes, 2 * tokens), F32),
        V((kept, lanes, hd), F32), V((kept, lanes, 128), F32), V((kept, lanes, 128), F32),
        V((chips, lanes + 16, hd), BF16), V((chips, lanes + 16, hd), BF16), V((1, lanes + 16, hd), BF16),
        V((2, half + 8, hd), F32), V((half + 8, hd), F32), V((2, half, 128), F32), V((2, half, 128), F32),
        V((128, 128), F32), V((lanes, hd), F32), V((chips, 2 * rows, fh), BF16), V((rows * pages, fh), F32),
        V((rows * pages, cols), F32), V((2 * zs, zrows, cols), BF16), V((2 * zs, zrows, cols), BF16),
        D((9 + 2 * groups,)), D((pages,)), D((pages,)), D((2 * groups,)), D((2 * groups,)), D, D, D, D,
        D((chips,)), D((chips,)), D((chips,)), D((chips,)), D((2 * zs,)), D((2 * zs,)),
    ]
    dims = (rows, per_kv, hd, tokens, groups, sufp)
    return pl.pallas_call(
        functools.partial(kernel, pages, zs, (side, chips // side), dims),
        out_shape=jax.ShapeDtypeStruct((zrows, cols), BF16),
        in_specs=[anym] * 9,
        out_specs=pl.BlockSpec(memory_space=pltpu.VMEM),
        scratch_shapes=scratch,
        compiler_params=pltpu.CompilerParams(
            collective_id=0, has_side_effects=True, vmem_limit_bytes=56 * 1024 * 1024),
    )(gid, slen, tab, queries, pk, pv, sk, sv, w)


def solution(mesh):
    placed = (
        P("page", "kvh", None), P(), P("page"), P("page", None),
        P(None, "page", "kvh", None), P(None, "page", "kvh", None),
        P("page", None, "kvh", None), P("page", None, "kvh", None), P("kvh", "page"),
    )
    return jax.shard_map(
        functools.partial(on_device, mesh.shape["page"], mesh.shape["kvh"]),
        mesh=mesh, in_specs=placed, out_specs=P("kvh", "page"), check_vma=False)
```

```python
import functools
import math

import jax
import jax.numpy as jnp
from jax import lax
from jax.experimental import pallas as pl
from jax.experimental.pallas import tpu as pltpu
from jax.sharding import PartitionSpec as P

MESH = pl.DeviceIdType.MESH
F32 = jnp.float32
BF16 = jnp.bfloat16
LOW = -1e30


def nt_dot(a, b):
    return lax.dot_general(a, b, (((1,), (1,)), ((), ())), preferred_element_type=F32)


def kernel(
    pages, zs, sides, dims,
    gid_in, slen_in, tab_in, q_in, pk, pv, sk, sv, w_in, out,
    gid, slen, tab, qv, q_all, kraw, vraw, stage, kd, vd, kr, vr, skv, svv, wl, wr, s_ref,
    acc_s, m_s, l_s, sendb, recvb, own_part, sfx, sfx_in, smc, slc, coef, fin, attn_all, a_mat, pf, part, pin,
    loc, q_ss, q_rs, kv_ss, kv_rs, w_ss, w_rs, x_ss, x_rs, o_ss, o_rs, a_ss, a_rs, p_ss, p_rs,
):
    rows, per_kv, hd, tokens, groups, sufp = dims
    chips = pages // 2
    lanes = 2 * rows * per_kv
    c2 = hd ** (-0.5) * math.log2(math.e)
    me = lax.axis_index("page")
    z = lax.axis_index("kvh")
    chip = me // 2
    core = me % 2
    other = 1 - core
    sib = chip * 2 + other
    sx, sy = sides
    cx, cy = chip // sy, chip % sy
    far_first = sorted(range(1, chips), key=lambda k: -min(k // sy, sx - k // sy) - min(k % sy, sy - k % sy))

    def chip_at(dx, dy):
        return (cx + dx) % sx * sy + (cy + dy) % sy

    def peer(j):
        k = jnp.int32(0)
        for i, v in enumerate(far_first):
            k = jnp.where(j == i, v, k)
        return chip_at(k // sy, k % sy)

    def to_page(src, dst, ss, rs, page):
        return pltpu.make_async_remote_copy(
            src_ref=src, dst_ref=dst, send_sem=ss, recv_sem=rs,
            device_id={"page": page}, device_id_type=MESH)

    bar = pltpu.get_barrier_semaphore()

    @pl.loop(1, pages)
    def _(j):
        pl.semaphore_signal(bar, inc=1, device_id={"page": (me + j) % pages}, device_id_type=MESH)

    @pl.loop(1, zs)
    def _(j):
        for cc in range(2):
            pl.semaphore_signal(
                bar, inc=1, device_id={"kvh": (z + j) % zs, "page": chip * 2 + cc}, device_id_type=MESH)

    loads = [
        pltpu.make_async_copy(q_in, qv, loc.at[0]),
        pltpu.make_async_copy(sk, skv, loc.at[1]),
        pltpu.make_async_copy(sv, svv, loc.at[2]),
        pltpu.make_async_copy(w_in.at[pl.ds(core * wl.shape[0], wl.shape[0])], wl, loc.at[3]),
        pltpu.make_async_copy(q_in.at[:, pl.ds(core * per_kv, per_kv)], q_all.at[chip, core], loc.at[4]),
    ]
    kvl = []
    for g in range(groups):
        kvl.append(pltpu.make_async_copy(pk.at[g], kraw.at[g], loc.at[6 + 2 * g]))
        kvl.append(pltpu.make_async_copy(pv.at[g], vraw.at[g], loc.at[7 + 2 * g]))
    small = [
        pltpu.make_async_copy(src, dst, loc.at[6 + 2 * groups + i])
        for i, (src, dst) in enumerate(((gid_in, gid), (slen_in, slen), (tab_in, tab)))]
    for copy in small + [loads[0], loads[4]] + kvl + loads[1:4]:
        copy.start()

    loads[0].wait()
    pl.semaphore_wait(bar, pages - 1 + 2 * (zs - 1))

    def q_copy(page, src_page):
        kv = page % 2
        return to_page(
            qv.at[:, pl.ds(kv * per_kv, per_kv)], q_all.at[src_page // 2, src_page % 2],
            q_ss.at[page], q_rs.at[src_page], page)

    for k in far_first:
        for cc in range(2):
            q_copy(chip_at(k // sy, k % sy) * 2 + cc, me).start()
    q_copy(sib, me).start()

    for copy in small:
        copy.wait()

    def count(r, c):
        g = gid[r]
        return tuple(c[e] + (g <= e).astype(jnp.int32) for e in range(groups - 1))

    first = lax.fori_loop(0, rows * pages, count, (jnp.int32(0),) * (groups - 1))
    btile = [jnp.minimum(f // (2 * rows), chips - 1) for f in first]

    def kv_copy(g, i):
        return to_page((kd, vd)[i].at[g, other], (kr, vr)[i].at[g], kv_ss.at[2 * g + i], kv_rs.at[2 * g + i], sib)

    for g in range(groups):
        for i in range(2):
            kvl[2 * g + i].wait()
            stage[...] = (kraw, vraw)[i][g].astype(F32)
            for kv in range(2):
                (kd, vd)[i][g, kv] = stage[pl.ds(kv, tokens, stride=2), :].astype(BF16)
            kv_copy(g, i).start()

    def w_copy():
        return to_page(w_in.at[pl.ds(other * wl.shape[0], wl.shape[0])], wr, w_ss, w_rs, sib)

    span = sufp * skv.shape[1]
    both = 2 * per_kv
    col = lax.broadcasted_iota(jnp.int32, (both, span), 1)
    row = lax.broadcasted_iota(jnp.int32, (both, span), 0)
    mine = (col % 2) == (row // per_kv)
    token = col // 2
    for copy in loads[1:3]:
        copy.wait()
    for r in range(rows):
        pgs = [tab[r, j] % skv.shape[0] for j in range(sufp)]
        keys = jnp.concatenate([skv[pg] for pg in pgs], axis=0)
        vals = jnp.concatenate([svv[pg] for pg in pgs], axis=0)
        live = mine & (token < slen[r])
        s = jnp.where(live, nt_dot(qv[r], keys) * c2, LOW)
        top = jnp.max(s, axis=1, keepdims=True)
        p = jnp.where(live, jnp.exp2(s - top), 0.0)
        tot = jnp.sum(p, axis=1, keepdims=True)
        o = jnp.dot(p.astype(BF16), vals, preferred_element_type=F32)
        for kv in range(2):
            a, b = kv * per_kv, (kv + 1) * per_kv
            sfx[kv, r * per_kv:(r + 1) * per_kv, :] = o[a:b]
            smc[kv, r * per_kv:(r + 1) * per_kv, :] = jnp.broadcast_to(top[a:b], (per_kv, 128))
            slc[kv, r * per_kv:(r + 1) * per_kv, :] = jnp.broadcast_to(tot[a:b], (per_kv, 128))
    half = rows * per_kv
    hrow = lax.broadcasted_iota(jnp.int32, (half, 128), 0) + core * half
    hlane = lax.broadcasted_iota(jnp.int32, (half, 128), 1)
    sub8 = lax.broadcasted_iota(jnp.int32, (8, 128), 0)
    lane8 = lax.broadcasted_iota(jnp.int32, (8, 128), 1)
    held = (lane8 // half) == core
    for kv in range(2):
        mrow = jnp.sum(jnp.where(hrow == hlane, smc[kv], 0.0), axis=0, keepdims=True)
        lrow = jnp.sum(jnp.where(hrow == hlane, slc[kv], 0.0), axis=0, keepdims=True)
        block = jnp.where(sub8 == 0, mrow, jnp.where(sub8 == 1, lrow, 0.0))
        sfx[kv, half:half + 8, :] = jnp.where(held, block, jnp.where(sub8 == 0, LOW, 0.0))

    def x_copy():
        return to_page(sfx.at[other], sfx_in, x_ss, x_rs, sib)

    x_copy().start()

    loads[4].wait()

    @pl.loop(1, pages)
    def _(j):
        q_copy(me, (me + j) % pages).wait_recv()

    for g in range(groups):
        for i in range(2):
            kv_copy(g, i).wait_recv()

    w_copy().start()

    def o_copy(dst_chip, src_chip):
        return to_page(sendb.at[dst_chip], recvb.at[src_chip], o_ss.at[dst_chip], o_rs.at[src_chip], dst_chip * 2 + core)

    prow = lax.broadcasted_iota(jnp.int32, (lanes, 128), 0)
    plane = lax.broadcasted_iota(jnp.int32, (lanes, 128), 1)
    nb = groups - 1

    def tile_of(k):
        t = peer(k)
        return t, gid[t * (2 * rows)]

    def columns(f, x):
        return functools.reduce(f, [x[:, i * 128:(i + 1) * 128] for i in range(tokens // 128)] if tokens > 128 else [x])

    def advance(now, then, slot, top_in):
        if now is not None:
            top = (jnp.max(top_in, axis=1, keepdims=True) * c2).astype(BF16).astype(F32)
        if then is not None:
            q = q_all[then[0]].reshape(lanes, hd)
        o, tot, top_out = None, None, None
        for i in range(2):
            part_of = slice(i * tokens, (i + 1) * tokens)
            if then is not None:
                x = nt_dot(q, kr[then[1]] if i else kd[then[1], core])
                s_ref[1 - slot, :, part_of] = x
                m = columns(jnp.maximum, x)
                top_out = m if i == 0 else jnp.maximum(top_out, m)
            if now is not None:
                p = jnp.exp2(s_ref[slot, :, part_of] * c2 - top)
                l = columns(jnp.add, p)
                tot = l if i == 0 else tot + l
                d = jnp.dot(p.astype(BF16), vr[now] if i else vd[now, core], preferred_element_type=F32)
                o = d if i == 0 else o + d
        if now is None:
            return top_out
        return top_out, o, top, jnp.sum(tot, axis=1, keepdims=True)

    def keep(at, o, top, tot):
        acc_s[at] = o
        m_s[at] = jnp.broadcast_to(top, (lanes, 128))
        l_s[at] = jnp.broadcast_to(tot, (lanes, 128))

    def finish(k, dst, at):
        t, g_low = tile_of(k)
        mc, lc = [], []
        for r in range(2 * rows):
            g_r = gid[t * (2 * rows) + r]
            src = jnp.where(g_r == g_low, nb, jnp.maximum(g_r - 1, 0))
            a, b = r * per_kv, (r + 1) * per_kv
            dst[at, a:b, :] = acc_s[src, a:b, :].astype(BF16)
            mc.append(m_s[src, a:b, :])
            lc.append(l_s[src, a:b, :])
        mrow = jnp.sum(jnp.where(prow == plane, jnp.concatenate(mc, axis=0), 0.0), axis=0, keepdims=True)
        lrow = jnp.sum(jnp.where(prow == plane, jnp.concatenate(lc, axis=0), 0.0), axis=0, keepdims=True)
        high = lrow.astype(BF16).astype(F32)
        sub = lax.broadcasted_iota(jnp.int32, (16, 128), 0)
        block = jnp.where(sub == 0, mrow, jnp.where(sub == 1, high, jnp.where(sub == 2, lrow - high, 0.0)))
        dst[at, lanes:lanes + 16, :] = block.astype(BF16)

    top = advance(None, (btile[0], 1), 1, None)
    for e in range(nb):
        then = (btile[e + 1], e + 2) if e + 1 < nb else tile_of(0)
        top, *res = advance(e + 1, then, e % 2, top)
        keep(e, *res)
    base = nb % 2

    def one(k, slot, top, last=False):
        t, g = tile_of(k)
        top, *res = advance(g, None if last else tile_of(k + 1), slot, top)
        keep(nb, *res)
        if last:
            finish(k, own_part, 0)
        else:
            finish(k, sendb, t)
            o_copy(t, chip).start()
        return top

    def pair(i, top):
        return one(2 * i + 1, 1 - base, one(2 * i, base, top))

    top = lax.fori_loop(0, chips // 2 - 1, pair, top)
    top = one(chips - 2, base, top)
    one(chips - 1, 1 - base, top, last=True)

    x_copy().wait_recv()

    @pl.loop(1, chips)
    def _(j):
        o_copy(chip, (chip + j) % chips).wait_recv()

    def partial(i, part_rows):
        return (recvb[(chip + i) % chips, part_rows, :] if i else own_part[0, part_rows, :]).astype(F32)

    ms, ls = [], []
    for i in range(chips):
        block = partial(i, slice(lanes, lanes + 16))
        ms.append(block[0:1])
        ls.append(block[1:2] + block[2:3])
    for block in (sfx[core, half:half + 8, :], sfx_in[half:half + 8, :]):
        ms.append(block[0:1])
        ls.append(block[1:2])
    peak = functools.reduce(jnp.maximum, ms)
    ws = [jnp.exp2(m - peak) for m in ms]
    inv = 1.0 / sum(a * b for a, b in zip(ws, ls))
    coef[...] = jnp.zeros_like(coef)
    for i, a in enumerate(ws):
        coef[i:i + 1, :] = a * inv
    ct = coef[...].T
    acc = jnp.zeros((lanes, hd), F32)
    for i in range(chips):
        acc += ct[:, i:i + 1] * partial(i, slice(0, lanes))
    fin[...] = acc
    mo = pl.ds(pl.multiple_of(core * half, half), half)
    so = pl.ds(pl.multiple_of(other * half, half), half)
    smc[0] = jnp.where(core == 0, ct[:half, chips:chips + 1], ct[half:, chips:chips + 1]) * sfx[core, :half, :]
    smc[1] = jnp.where(core == 0, ct[half:, chips + 1:chips + 2], ct[:half, chips + 1:chips + 2]) * sfx_in[:half, :]
    fin[mo, :] += smc[0]
    fin[so, :] += smc[1]
    for h in range(per_kv):
        attn_all[chip, :, h * hd:(h + 1) * hd] = fin[pl.ds(h, 2 * rows, stride=per_kv), :].astype(BF16)

    def a_copy(dst_chip, src_chip):
        return to_page(
            attn_all.at[src_chip], attn_all.at[src_chip], a_ss.at[dst_chip], a_rs.at[src_chip], dst_chip * 2 + core)

    for k in far_first:
        a_copy(chip_at(k // sy, k % sy), chip).start()

    @pl.loop(1, pages)
    def _(j):
        q_copy((me + j) % pages, me).wait_send()

    for g in range(groups):
        for i in range(2):
            kv_copy(g, i).wait_send()
    w_copy().wait_send()
    x_copy().wait_send()

    @pl.loop(1, chips)
    def _(j):
        o_copy((chip + j) % chips, chip).wait_send()

    loads[3].wait()
    w_copy().wait_recv()
    zrows = out.shape[0]
    pin[z * 2 + core] = jnp.zeros(pin.shape[1:], BF16)

    @pl.loop(1, chips)
    def _(j):
        a_copy(chip, (chip + j) % chips).wait_recv()

    for i in range(chips // 2):
        pair = jnp.concatenate([attn_all[2 * i].astype(F32), attn_all[2 * i + 1].astype(F32)], axis=0)
        a_mat[i * 4 * rows:(i + 1) * 4 * rows, :] = pair.astype(BF16)

    def p_copy(dst_z, dst_core, src_z, src_core):
        return pltpu.make_async_remote_copy(
            src_ref=part.at[dst_z * 2 + dst_core], dst_ref=pin.at[src_z * 2 + src_core],
            send_sem=p_ss.at[dst_z * 2 + dst_core], recv_sem=p_rs.at[src_z * 2 + src_core],
            device_id={"kvh": dst_z, "page": chip * 2 + dst_core}, device_id_type=MESH)

    y = jnp.dot(a_mat[...], wr[...], preferred_element_type=F32)
    for k in range(zs):
        part[k * 2 + other] = y[k * zrows:(k + 1) * zrows].astype(BF16)

    @pl.loop(0, zs)
    def _(j):
        p_copy((z + j) % zs, other, z, core).start()

    y = jnp.dot(a_mat[...], wl[...], preferred_element_type=F32)
    pf[...] = y
    for k in range(zs):
        part[k * 2 + core] = y[k * zrows:(k + 1) * zrows].astype(BF16)

    @pl.loop(1, zs)
    def _(j):
        p_copy((z + j) % zs, core, z, core).start()

    @pl.loop(1, chips)
    def _(j):
        a_copy((chip + j) % chips, chip).wait_send()

    @pl.loop(0, zs)
    def _(j):
        p_copy(z, core, (z + j) % zs, other).wait_recv()

    @pl.loop(1, zs)
    def _(j):
        p_copy(z, core, (z + j) % zs, core).wait_recv()

    total = pf[pl.ds(pl.multiple_of(z * zrows, zrows), zrows), :]
    for i in range(2 * zs):
        total += pin[i].astype(F32)
    out[...] = total.astype(BF16)

    @pl.loop(0, zs)
    def _(j):
        p_copy((z + j) % zs, other, z, core).wait_send()

    @pl.loop(1, zs)
    def _(j):
        p_copy((z + j) % zs, core, z, core).wait_send()


def on_device(pages, zs, queries, gid, slen, tab, pk, pv, sk, sv, w):
    rows, heads, hd = queries.shape
    groups, tokens, kvs = pk.shape[:3]
    per_kv = heads // kvs
    pool, plen = sk.shape[:2]
    sufp = tab.shape[1]
    chips = pages // 2
    side = math.isqrt(chips)
    side = side if side * side == chips else 1
    lanes = 2 * rows * per_kv
    half = rows * per_kv
    feats, cols = w.shape
    fh = feats // 2
    zrows = rows * pages // zs
    pk = pk.reshape(groups, tokens * kvs, hd)
    pv = pv.reshape(groups, tokens * kvs, hd)
    sk = sk.reshape(pool, plen * kvs, hd)
    sv = sv.reshape(pool, plen * kvs, hd)
    V, D = pltpu.VMEM, pltpu.SemaphoreType.DMA
    anym = pl.BlockSpec(memory_space=pl.ANY)
    scratch = [
        pltpu.SMEM(gid.shape, jnp.int32), pltpu.SMEM(slen.shape, jnp.int32), pltpu.SMEM(tab.shape, jnp.int32),
        V((rows, heads, hd), BF16), V((chips, 2, rows, per_kv, hd), BF16),
        V((groups, 2 * tokens, hd), BF16), V((groups, 2 * tokens, hd), BF16), V((2 * tokens, hd), F32),
        V((groups, 2, tokens, hd), BF16), V((groups, 2, tokens, hd), BF16),
        V((groups, tokens, hd), BF16), V((groups, tokens, hd), BF16),
        V((pool, plen * kvs, hd), BF16), V((pool, plen * kvs, hd), BF16),
        V((fh, cols), BF16), V((fh, cols), BF16), V((2, lanes, 2 * tokens), F32),
        V((groups, lanes, hd), F32), V((groups, lanes, 128), F32), V((groups, lanes, 128), F32),
        V((chips, lanes + 16, hd), BF16), V((chips, lanes + 16, hd), BF16), V((1, lanes + 16, hd), BF16),
        V((2, half + 8, hd), F32), V((half + 8, hd), F32), V((2, half, 128), F32), V((2, half, 128), F32),
        V((128, 128), F32), V((lanes, hd), F32), V((chips, 2 * rows, fh), BF16), V((rows * pages, fh), BF16),
        V((rows * pages, cols), F32), V((2 * zs, zrows, cols), BF16), V((2 * zs, zrows, cols), BF16),
        D((9 + 2 * groups,)), D((pages,)), D((pages,)), D((2 * groups,)), D((2 * groups,)), D, D, D, D,
        D((chips,)), D((chips,)), D((chips,)), D((chips,)), D((2 * zs,)), D((2 * zs,)),
    ]
    dims = (rows, per_kv, hd, tokens, groups, sufp)
    return pl.pallas_call(
        functools.partial(kernel, pages, zs, (side, chips // side), dims),
        out_shape=jax.ShapeDtypeStruct((zrows, cols), BF16),
        in_specs=[anym] * 9,
        out_specs=pl.BlockSpec(memory_space=pltpu.VMEM),
        scratch_shapes=scratch,
        compiler_params=pltpu.CompilerParams(
            collective_id=0, has_side_effects=True, vmem_limit_bytes=56 * 1024 * 1024),
    )(gid, slen, tab, queries, pk, pv, sk, sv, w)


def solution(mesh):
    placed = (
        P("page", "kvh", None), P(), P("page"), P("page", None),
        P(None, "page", "kvh", None), P(None, "page", "kvh", None),
        P("page", None, "kvh", None), P("page", None, "kvh", None), P("kvh", "page"),
    )
    return jax.shard_map(
        functools.partial(on_device, mesh.shape["page"], mesh.shape["kvh"]),
        mesh=mesh, in_specs=placed, out_specs=P("kvh", "page"), check_vma=False)
```
